128 devices in a mesh: bulk: 8 (over x, core), valve: 16 (over z, y).
Axes of the slice: x: 4, y: 4, z: 4, core: 2. Of those that a mesh axis runs over, the one named last changes fastest.
Arguments:
- bg_adjoint: float32 [5, 64, 512, 128], P(None, 'bulk', 'valve'), may hold values from -6 to 6
- bg_velocity: float32 [3, 64, 512, 128], P(None, 'bulk', 'valve'), may hold values from -6 to 6
- bg_source: float32 [5, 64, 512, 128], P(None, 'bulk', 'valve'), may hold values from -6 to 6
- bg_iblank: int32 [64, 512, 128], P('bulk', 'valve'), may hold values 0 or 1
- valve_adjoint: float32 [5, 128, 256, 128], P(None, 'valve', 'bulk'), may hold values from -6 to 6
- valve_velocity: float32 [3, 128, 256, 128], P(None, 'valve', 'bulk'), may hold values from -6 to 6
- valve_source: float32 [5, 128, 256, 128], P(None, 'valve', 'bulk'), may hold values from -6 to 6
- flux_mix: float32 [3, 5, 5], replicated, may hold values from -2.5 to 2.5
- rec_cell: int32 [128, 128, 128], P(('bulk', 'valve')), may hold values from 0 to 32767
- donor_base: int32 [128, 128, 128], P(('bulk', 'valve')), may hold values from 0 to 28542, as said below
- donor_weight: float32 [8, 128, 128, 128], P(None, ('bulk', 'valve')), may hold values from 0 to 1, as said below
- slot_count: int32 [128, 128], P(('bulk', 'valve')), may hold values from 0 to 128, as said below
Outputs:
- bg_out: float32 [5, 64, 512, 128], P(None, 'bulk', 'valve')
- valve_out: float32 [5, 128, 256, 128], P(None, 'valve', 'bulk')
The draws below stay inside these ranges and needn't reach their ends.
Inputs may be any that keep to these rules, and one draw needn't show every extreme that they name: donor_base is a cell of the block whose neighbours at +1 along each of the three dimensions, alone and together, are in the same block; both ends of the range occur in every draw. `donor_weight`: the eight weights of a slot are non-negative and sum to one. `slot_count`: some owner takes 128 live slots from every sender.
All inputs are finite; a program needn't handle non-finite values. No bound on the sum of `bg_iblank` on one device may be relied on, other than what follows from the above.
Results may differ from the reference program's by a relative error of at most 0.0001.
Values sent between devices are 32-bit elements; how exact they have to be, the bound alone decides.
A program may use at most 128 MiB of HBM per device.

```python
import jax
import jax.numpy as jnp
from jax import lax

NVAR = 5
ITERS = 4
CAP = 128
BX = 8
BY = 32
BZ = 128
VX = 8
VY = 32
VZ = 128
NBX = 64
NBY = 512
NVX = 128
NVY = 256
BCELLS = 32768
VCELLS = 32768
N_BULK = 8
N_VALVE = 16


def draw_donor_base(key, part):
    devices = N_BULK * N_VALVE
    first, second, third = jax.random.split(jax.random.fold_in(key, 11), 3)
    shape = (devices, devices, CAP)
    along_x = jax.random.randint(first, shape, 0, BX - 1)
    along_y = jax.random.randint(second, shape, 0, BY - 1)
    along_z = jax.random.randint(third, shape, 0, BZ - 1)
    flat = (along_x * BY + along_y) * BZ + along_z
    highest = ((BX - 2) * BY + BY - 2) * BZ + BZ - 2
    owners = jnp.arange(devices, dtype=jnp.int32)[None, :, None]
    slots = jnp.arange(CAP, dtype=jnp.int32)[None, None, :]
    last_slot = slots == CAP - 1
    flat = jnp.where(last_slot & (owners == 0), highest, flat)
    flat = jnp.where(last_slot & (owners == 1), 0, flat)
    return flat.astype(jnp.int32)


def draw_donor_weight(key, part):
    devices = N_BULK * N_VALVE
    fractions = jax.random.uniform(jax.random.fold_in(key, 23), (3, devices, devices, CAP), jnp.float32)
    weights = []
    for corner in range(8):
        picks = (corner // 4, corner // 2 % 2, corner % 2)
        factor = jnp.ones((devices, devices, CAP), jnp.float32)
        for direction in range(3):
            part_frac = fractions[direction]
            factor = factor * (part_frac if picks[direction] == 1 else 1.0 - part_frac)
        weights.append(factor)
    return jnp.stack(weights, axis=0).astype(jnp.float32)


def draw_slot_count(key, part):
    devices = N_BULK * N_VALVE
    first, second, third = jax.random.split(jax.random.fold_in(key, 37), 3)
    raw_counts = jax.random.randint(first, (devices, devices), 0, CAP + 1)
    loading = jax.random.randint(second, (devices,), 2, 5)
    counts = raw_counts * loading[None, :] // 4
    hottest = jax.random.randint(third, (), 0, devices)
    owners = jnp.arange(devices, dtype=jnp.int32)[None, :]
    return jnp.where(owners == hottest, CAP, counts).astype(jnp.int32)


def touch_ends(drawn, key, smallest, top_value):
    dims = drawn.shape
    index_at = [jax.random.randint(jax.random.fold_in(key, axis), (), 0, dims[axis]) for axis in range(len(dims))]
    drawn = drawn.at[tuple(index_at)].set(smallest)
    longest = dims.index(max(dims))
    index_at[longest] = (index_at[longest] + 1) % dims[longest]
    return drawn.at[tuple(index_at)].set(top_value)


def levels(key, extent, shards, least, top_value):
    gain, own = 1.0, jax.random.fold_in(key, 6)
    for axis_at, blocks in shards:
        heights = jnp.exp(jax.random.uniform(jax.random.fold_in(own, axis_at), (blocks,), jnp.float32, least / len(shards), top_value / len(shards)))
        gain = gain * jnp.repeat(heights, extent[axis_at] // blocks).reshape([-1 if axis == axis_at else 1 for axis in range(len(extent))])
    return gain


def centred(rng, extent, width, bound, pieces=(), kind=jnp.bfloat16):
    values = width * jax.random.normal(rng, extent, jnp.float32)
    if pieces:
        values = values * levels(rng, extent, pieces, -0.22, 0.18)
    return jnp.clip(values, -bound, bound).astype(kind)


def setup_inputs(seed: int = 0) -> dict:
    arg_keys = jax.random.split(jax.random.key(seed), 13)
    bg_adjoint = centred(arg_keys[0], (NVAR, NBX, NBY, BZ), 1.0, 6.0, ((1, 8), (2, 16)), jnp.float32)
    bg_velocity = centred(arg_keys[1], (3, NBX, NBY, BZ), 1.0, 6.0, ((1, 8), (2, 16)), jnp.float32)
    bg_source = centred(arg_keys[2], (NVAR, NBX, NBY, BZ), 1.0, 6.0, ((1, 8), (2, 16)), jnp.float32)
    bg_iblank = touch_ends((jax.random.randint(arg_keys[3], (NBX, NBY, BZ), 0, 8) < 7).astype(jnp.int32), jax.random.fold_in(arg_keys[3], 1), 0, 1)
    valve_adjoint = centred(arg_keys[4], (NVAR, NVX, NVY, VZ), 1.0, 6.0, ((1, 16), (2, 8)), jnp.float32)
    valve_velocity = centred(arg_keys[5], (3, NVX, NVY, VZ), 1.0, 6.0, ((1, 16), (2, 8)), jnp.float32)
    valve_source = centred(arg_keys[6], (NVAR, NVX, NVY, VZ), 1.0, 6.0, ((1, 16), (2, 8)), jnp.float32)
    flux_mix = centred(arg_keys[7], (3, NVAR, NVAR), NVAR ** -0.5, 2.5, (), jnp.float32)
    rec_cell = touch_ends(jax.random.randint(arg_keys[8], (N_BULK * N_VALVE, N_BULK * N_VALVE, CAP), 0, VX * VY * VZ), jax.random.fold_in(arg_keys[8], 1), 0, (VX * VY * VZ) - 1).astype(jnp.int32)
    donor_base = draw_donor_base(jax.random.fold_in(arg_keys[12], 71), 0)
    donor_weight = draw_donor_weight(jax.random.fold_in(arg_keys[12], 71), 0)
    slot_count = draw_slot_count(jax.random.fold_in(arg_keys[12], 71), 0)
    return dict(bg_adjoint=bg_adjoint, bg_velocity=bg_velocity, bg_source=bg_source, bg_iblank=bg_iblank, valve_adjoint=valve_adjoint, valve_velocity=valve_velocity, valve_source=valve_source, flux_mix=flux_mix, rec_cell=rec_cell, donor_base=donor_base, donor_weight=donor_weight, slot_count=slot_count)


def slopes_of(velocity):
    inverse_speed = lax.rsqrt(1.0 + lax.optimization_barrier(jnp.sum(velocity * velocity, axis=0)))
    return velocity * inverse_speed[None]

def update_cells(padded, slopes, source, blanking, flux_mix):
    beside_all = padded[:, 2:, 1:-1, 1:-1] + padded[:, :-2, 1:-1, 1:-1]
    beside_all = beside_all + padded[:, 1:-1, 2:, 1:-1] + padded[:, 1:-1, :-2, 1:-1]
    beside_all = beside_all + padded[:, 1:-1, 1:-1, 2:] + padded[:, 1:-1, 1:-1, :-2]
    centrals = (padded[:, :-2, 1:-1, 1:-1] - padded[:, 2:, 1:-1, 1:-1], padded[:, 1:-1, :-2, 1:-1] - padded[:, 1:-1, 2:, 1:-1], padded[:, 1:-1, 1:-1, :-2] - padded[:, 1:-1, 1:-1, 2:])
    transposed = jnp.zeros_like(beside_all)
    for direction in range(3):
        mixed = jnp.einsum('ji,jxyz->ixyz', flux_mix[direction], centrals[direction], precision=lax.Precision.HIGHEST)
        transposed = transposed + slopes[direction][None] * (0.5 * mixed)
    return blanking * (beside_all - transposed + source) / 12.0

def sweep_grid(adjoint, velocity, source, blanking, flux_mix):
    slopes = slopes_of(velocity)
    for repeat in range(ITERS):
        padded = jnp.pad(adjoint, ((0, 0), (1, 1), (1, 1), (1, 1)))
        adjoint = update_cells(padded, slopes, source, blanking, flux_mix)
    return adjoint

def reference(bg_adjoint, bg_velocity, bg_source, bg_iblank, valve_adjoint, valve_velocity, valve_source, flux_mix, rec_cell, donor_base, donor_weight, slot_count):
    devices = N_BULK * N_VALVE
    valve_out = sweep_grid(valve_adjoint, valve_velocity, valve_source, 1.0, flux_mix)
    blocks = valve_out.reshape(NVAR, N_VALVE, VX, N_BULK, VY, VZ).transpose(3, 1, 0, 2, 4, 5).reshape(devices, NVAR, VCELLS)
    values = jax.vmap(lambda block, chosen: block[:, chosen])(blocks, rec_cell)
    valid = (jnp.arange(CAP, dtype=jnp.int32)[None, None, :] < slot_count[:, :, None]).astype(jnp.float32)
    active = values * valid[:, None]
    owner_start = jnp.arange(devices, dtype=jnp.int32)[None, :, None] * BCELLS
    pushed = jnp.zeros((NVAR, devices * BCELLS), jnp.float32)
    for corner in range(8):
        step_x, step_y, step_z = (corner // 4, corner // 2 % 2, corner % 2)
        offset = step_x * BY * BZ + step_y * BZ + step_z
        target = (owner_start + donor_base + offset).reshape(-1).astype(jnp.int32)
        contrib = donor_weight[corner][:, None] * active
        pushed = pushed.at[:, target].add(contrib.transpose(1, 0, 2, 3).reshape(NVAR, -1))
    pushed = pushed.reshape(NVAR, N_BULK, N_VALVE, BX, BY, BZ).transpose(0, 1, 3, 2, 4, 5).reshape(NVAR, NBX, NBY, BZ)
    blanking = bg_iblank.astype(jnp.float32)[None]
    bg_out = sweep_grid(bg_adjoint, bg_velocity, bg_source, blanking, flux_mix) + pushed
    return (bg_out, valve_out)
```

```python
import functools

import jax
import jax.numpy as jnp
from jax import lax
from jax.experimental import pallas as pl
from jax.experimental.pallas import tpu as pltpu
from jax.sharding import PartitionSpec as P

NVAR = 5
ITERS = 4
CAP = 128
BX = 8
BY = 32
BZ = 128
PLANES = BX * BY
GROUP = 16

f32 = jnp.float32
bf16 = jnp.bfloat16
NT = (((1,), (1,)), ((), ()))
NN = (((1,), (0,)), ((), ()))


def extended(block, sides, width):
    for axis, dim in sides:
        count = lax.axis_size(axis)
        forward = [(i, i + 1) for i in range(count - 1)]
        backward = [(target, source) for source, target in forward]
        low = lax.ppermute(
            lax.slice_in_dim(block, block.shape[dim] - width, None, axis=dim), axis, forward
        )
        high = lax.ppermute(lax.slice_in_dim(block, 0, width, axis=dim), axis, backward)
        block = jnp.concatenate([low, block, high], axis=dim)
    return block


def slopes_of(velocity):
    inverse_speed = lax.rsqrt(1.0 + jnp.sum(velocity * velocity, axis=0))
    return velocity * inverse_speed[None]


def update_cells(padded, slopes, source, blanking, flux_mix):
    beside_all = padded[:, 2:, 1:-1, 1:-1] + padded[:, :-2, 1:-1, 1:-1]
    beside_all = beside_all + padded[:, 1:-1, 2:, 1:-1] + padded[:, 1:-1, :-2, 1:-1]
    beside_all = beside_all + padded[:, 1:-1, 1:-1, 2:] + padded[:, 1:-1, 1:-1, :-2]
    centrals = (
        padded[:, :-2, 1:-1, 1:-1] - padded[:, 2:, 1:-1, 1:-1],
        padded[:, 1:-1, :-2, 1:-1] - padded[:, 1:-1, 2:, 1:-1],
        padded[:, 1:-1, 1:-1, :-2] - padded[:, 1:-1, 1:-1, 2:],
    )
    transposed = jnp.zeros_like(beside_all)
    for direction in range(3):
        mixed = jnp.einsum(
            "ji,jxyz->ixyz",
            flux_mix[direction],
            centrals[direction],
            precision=lax.Precision.HIGHEST,
        )
        transposed = transposed + slopes[direction][None] * (0.5 * mixed)
    return blanking * (beside_all - transposed + source) / 12.0


def depth_pad(framed):
    return jnp.pad(framed, ((0, 0), (0, 0), (0, 0), (1, 1)))


def sweeps(adjoint, velocity, source, blanking, flux_mix, sides):
    slopes = slopes_of(velocity)
    for _ in range(ITERS):
        framed = extended(adjoint, sides, 1)
        adjoint = update_cells(depth_pad(framed), slopes, source, blanking, flux_mix)
    return adjoint


def split(x):
    hi = x.astype(bf16)
    return hi, (x - hi.astype(f32)).astype(bf16)


def as_bf16(x):
    return x.astype(f32).astype(bf16)


def pick_kernel(count_ref, cell_ref, field_ref, out_ref, table):
    for c in range(NVAR):
        hi, lo = split(field_ref[c].T)
        table[pl.ds(c * BZ, BZ), 0:PLANES] = hi
        table[pl.ds(c * BZ, BZ), PLANES : 2 * PLANES] = lo
    plane_row = as_bf16(lax.broadcasted_iota(jnp.int32, (PLANES, CAP), 0))
    depth_row = lax.broadcasted_iota(jnp.int32, (BZ, CAP), 0)
    slot = lax.broadcasted_iota(jnp.int32, (1, CAP), 1)
    one, zero = jnp.ones((), bf16), jnp.zeros((), bf16)

    def body(block, carry):
        hits, depths = [], []
        for u in range(GROUP):
            owner = block * GROUP + u
            cell = cell_ref[owner]
            hits.append(jnp.where(plane_row == as_bf16(cell >> 7), one, zero))
            depths.append(jnp.where(slot < count_ref[0, owner], cell & (BZ - 1), -1))
        hits = jnp.concatenate(hits, axis=1)
        columns = lax.dot_general(
            table[...], jnp.concatenate([hits, hits], axis=0), NN, preferred_element_type=f32
        )
        for u in range(GROUP):
            here = depth_row == depths[u]
            rows = [
                jnp.sum(
                    jnp.where(here, columns[c * BZ : (c + 1) * BZ, u * CAP : (u + 1) * CAP], 0.0),
                    axis=0,
                    keepdims=True,
                )
                for c in range(NVAR)
            ]
            out_ref[block * GROUP + u] = jnp.concatenate(rows + [jnp.zeros((3, CAP), f32)], axis=0)
        return carry

    lax.fori_loop(0, out_ref.shape[0] // GROUP, body, 0)


def pick(field, cells, counts):
    owners = cells.shape[0]
    return pl.pallas_call(
        pick_kernel,
        out_shape=jax.ShapeDtypeStruct((owners, 8, CAP), f32),
        in_specs=[
            pl.BlockSpec(memory_space=pltpu.SMEM),
            pl.BlockSpec(memory_space=pltpu.VMEM),
            pl.BlockSpec(memory_space=pltpu.VMEM),
        ],
        out_specs=pl.BlockSpec(memory_space=pltpu.VMEM),
        scratch_shapes=[pltpu.VMEM((NVAR * BZ, 2 * PLANES), bf16)],
        compiler_params=pltpu.CompilerParams(vmem_limit_bytes=56 * 2**20),
    )(counts, cells.reshape(owners, 1, CAP), field.reshape(NVAR, PLANES, BZ))


def push_kernel(value_ref, weight_ref, base_ref, field_ref, out_ref, total):
    total[...] = jnp.zeros_like(total)
    plane_row = as_bf16(lax.broadcasted_iota(jnp.int32, (PLANES, CAP), 0))
    depth_row = as_bf16(lax.broadcasted_iota(jnp.int32, (BZ, CAP), 0))
    zero = jnp.zeros((), bf16)

    def terms(sender):
        base = base_ref[sender]
        plane = base >> 7
        weight_hi, weight_lo = split(weight_ref[sender])
        value_hi, value_lo = split(value_ref[sender])
        hits = [plane_row == as_bf16(plane + off) for off in (0, 1, BY, BY + 1)]

        def spread(weight):
            halves = []
            for step in range(2):
                rows = jnp.zeros((PLANES, CAP), bf16)
                for pair in range(4):
                    rows = jnp.where(hits[pair], weight[2 * pair + step : 2 * pair + step + 1], rows)
                halves.append(rows)
            return jnp.concatenate(halves, axis=0)

        here = depth_row == as_bf16(base & (BZ - 1))

        def placed(value):
            return jnp.concatenate(
                [jnp.where(here, value[c : c + 1], zero) for c in range(NVAR)], axis=0
            )

        return spread(weight_hi), spread(weight_lo), placed(value_hi), placed(value_lo)

    def body(block, carry):
        parts = [terms(block * GROUP + u) for u in range(GROUP)]
        spread_hi, spread_lo, placed_hi, placed_lo = [[part[i] for part in parts] for i in range(4)]
        spread = jnp.concatenate(spread_hi + spread_hi + spread_lo, axis=1)
        placed = jnp.concatenate(placed_hi + placed_lo + placed_hi, axis=1)
        total[...] += lax.dot_general(placed, spread, NT, preferred_element_type=f32)
        return carry

    lax.fori_loop(0, base_ref.shape[0] // GROUP, body, 0)
    for c in range(NVAR):
        lower = total[pl.ds(c * BZ, BZ), 0:PLANES]
        upper = total[pl.ds(c * BZ, BZ), PLANES : 2 * PLANES]
        out_ref[c] = field_ref[c] + (lower + pltpu.roll(upper, 1, axis=0)).T


def push(values, weights, base, field):
    return pl.pallas_call(
        push_kernel,
        out_shape=jax.ShapeDtypeStruct((NVAR, PLANES, BZ), f32),
        in_specs=[pl.BlockSpec(memory_space=pltpu.VMEM)] * 4,
        out_specs=pl.BlockSpec(memory_space=pltpu.VMEM),
        scratch_shapes=[pltpu.VMEM((NVAR * BZ, 2 * PLANES), f32)],
        compiler_params=pltpu.CompilerParams(vmem_limit_bytes=56 * 2**20),
    )(values, weights, base, field.reshape(NVAR, PLANES, BZ))


def exchange(x):
    return lax.all_to_all(x, ("bulk", "valve"), split_axis=0, concat_axis=0, tiled=True)


def body(
    bg_adjoint,
    bg_velocity,
    bg_source,
    bg_iblank,
    valve_adjoint,
    valve_velocity,
    valve_source,
    flux_mix,
    rec_cell,
    donor_base,
    donor_weight,
    slot_count,
):
    weights = exchange(donor_weight[:, 0].transpose(1, 0, 2))
    base = exchange(donor_base[0][:, None, :])
    valve_out = sweeps(
        valve_adjoint, valve_velocity, valve_source, 1.0, flux_mix, (("bulk", 2), ("valve", 1))
    )
    values = exchange(pick(valve_out, rec_cell[0], slot_count))
    blanking = bg_iblank.astype(f32)[None]
    bg_swept = sweeps(
        bg_adjoint, bg_velocity, bg_source, blanking, flux_mix, (("bulk", 1), ("valve", 2))
    )
    bg_out = push(values, weights, base, bg_swept).reshape(bg_adjoint.shape)
    return (bg_out, valve_out)


def solution(mesh):
    placed = (
        P(None, "bulk", "valve", None),
        P(None, "bulk", "valve", None),
        P(None, "bulk", "valve", None),
        P("bulk", "valve", None),
        P(None, "valve", "bulk", None),
        P(None, "valve", "bulk", None),
        P(None, "valve", "bulk", None),
        P(),
        P(("bulk", "valve"), None, None),
        P(("bulk", "valve"), None, None),
        P(None, ("bulk", "valve"), None, None),
        P(("bulk", "valve"), None),
    )
    return jax.shard_map(
        body,
        mesh=mesh,
        in_specs=placed,
        out_specs=(P(None, "bulk", "valve", None), P(None, "valve", "bulk", None)),
        check_vma=False,
    )
```

```python
import functools

import jax
import jax.numpy as jnp
from jax import lax
from jax.experimental import pallas as pl
from jax.experimental.pallas import tpu as pltpu
from jax.sharding import PartitionSpec as P

NVAR = 5
ITERS = 4
CAP = 128
BX = 8
BY = 32
BZ = 128
PLANES = BX * BY
GROUP = 16

f32 = jnp.float32
bf16 = jnp.bfloat16
NT = (((1,), (1,)), ((), ()))
NN = (((1,), (0,)), ((), ()))
MESH = pl.DeviceIdType.MESH


def sweep_kernel(*refs):
    (flux_ref, valve_adj, valve_vel, valve_src, bg_adj, bg_vel, bg_src, bg_blank, valve_out, bg_out) = refs[:10]
    fields = (refs[10 : 10 + ITERS], refs[10 + ITERS : 10 + 2 * ITERS])
    (slopes, scale, edge_in, edge_out, load_sem, send_sem, recv_sem) = refs[10 + 2 * ITERS :]
    bulk, valve = lax.axis_index("bulk"), lax.axis_index("valve")
    n_bulk, n_valve = lax.axis_size("bulk"), lax.axis_size("valve")
    place = {"bulk": (bulk, n_bulk), "valve": (valve, n_valve)}
    axes = (("valve", "bulk"), ("bulk", "valve"))
    inputs = ((valve_adj, valve_vel, valve_src), (bg_adj, bg_vel, bg_src))
    outputs = (valve_out, bg_out)

    loads = [
        pltpu.make_async_copy(inputs[g][0], fields[g][0].at[:, pl.ds(1, BX)], load_sem.at[g])
        for g in range(2)
    ]
    for load in loads:
        load.start()

    def clear(g, side):
        index, count = place[axes[g][0]]

        @pl.when(index == (0 if side == 0 else count - 1))
        def _():
            for t in range(ITERS):
                fields[g][t][:, (BX + 1) * side] = jnp.zeros((NVAR, BY, BZ), f32)

        index, count = place[axes[g][1]]

        @pl.when(index == (0 if side == 0 else count - 1))
        def _():
            for t in range(ITERS):
                edge_in[g, t, side] = jnp.zeros((NVAR, BX, 1, BZ), f32)

    for g in range(2):
        for side in range(2):
            clear(g, side)

    barrier = pltpu.get_barrier_semaphore()
    for axis in ("bulk", "valve"):
        index, count = place[axis]
        for step in (1, count - 1):
            pl.semaphore_signal(
                barrier, inc=1, device_id={axis: lax.rem(index + step, count)}, device_id_type=MESH
            )

    def slope_rows(x, carry):
        for g in range(2):
            parts = [inputs[g][1][d, x] for d in range(3)]
            square = parts[0] * parts[0] + parts[1] * parts[1] + parts[2] * parts[2]
            half = 0.5 * lax.rsqrt(1.0 + square)
            for d in range(3):
                slopes[g, d, x] = parts[d] * half
        scale[x] = bg_blank[x].astype(f32) * (1.0 / 12.0)
        return carry

    def copies(g, t, side):
        away = 1 - side
        found = []
        for kind in range(2):
            index, count = place[axes[g][kind]]
            target = lax.rem(index + (1 if side else count - 1), count)
            if kind == 0:
                source = fields[g][t].at[:, BX if side else 1]
                landing = fields[g][t].at[:, 0 if side else BX + 1]
            else:
                source = edge_out.at[g, t, side]
                landing = edge_in.at[g, t, away]
            found.append(
                (
                    index < count - 1 if side else index > 0,
                    index > 0 if side else index < count - 1,
                    pltpu.make_async_remote_copy(
                        src_ref=source,
                        dst_ref=landing,
                        send_sem=send_sem.at[g, t, side, kind],
                        recv_sem=recv_sem.at[g, t, side, kind],
                        device_id={axes[g][kind]: target},
                        device_id_type=MESH,
                    ),
                )
            )
        return found

    def send(g, t):
        for side in range(2):
            for sends, _, copy in copies(g, t, side):
                pl.when(sends)(copy.start)

    def arrive(g, t):
        for side in range(2):
            for _, receives, copy in copies(g, t, side):
                pl.when(receives)(copy.wait_recv)

    def left(g, t):
        for side in range(2):
            for sends, _, copy in copies(g, t, side):
                pl.when(sends)(copy.wait_send)

    row = lax.broadcasted_iota(jnp.int32, (BY, BZ), 0)
    lane = lax.broadcasted_iota(jnp.int32, (BY, BZ), 1)

    def sweep(g, t):
        now = fields[g][t]
        source = inputs[g][2]

        def rows(x, carry):
            around, steep = [], [[], [], []]
            for c in range(NVAR):
                here = now[c, x + 1]
                x_low, x_high = now[c, x], now[c, x + 2]
                y_low = jnp.where(row == 0, edge_in[g, t, 0, c, x], pltpu.roll(here, 1, axis=0))
                y_high = jnp.where(row == BY - 1, edge_in[g, t, 1, c, x], pltpu.roll(here, BY - 1, axis=0))
                z_low = jnp.where(lane == 0, 0.0, pltpu.roll(here, 1, axis=1))
                z_high = jnp.where(lane == BZ - 1, 0.0, pltpu.roll(here, BZ - 1, axis=1))
                around.append(
                    (x_low + x_high) + (y_low + y_high) + (z_low + z_high) + source[c, x]
                )
                for d, (low, high) in enumerate(((x_low, x_high), (y_low, y_high), (z_low, z_high))):
                    steep[d].append(slopes[g, d, x] * (low - high))
            factor = scale[x] if g else 1.0 / 12.0
            for i in range(NVAR):
                total = around[i]
                for d in range(3):
                    for j in range(NVAR):
                        total = total - flux_ref[d, j, i] * steep[d][j]
                total = total * factor
                if t == ITERS - 1:
                    outputs[g][i, x] = total
                else:
                    fields[g][t + 1][i, x + 1] = total
                    edge_out[g, t + 1, 0, i, x] = total[0:1]
                    edge_out[g, t + 1, 1, i, x] = total[BY - 1 : BY]
            return carry

        lax.fori_loop(0, BX, rows, 0)

    def first_edges(g):
        def rows(x, carry):
            for c in range(NVAR):
                here = fields[g][0][c, x + 1]
                edge_out[g, 0, 0, c, x] = here[0:1]
                edge_out[g, 0, 1, c, x] = here[BY - 1 : BY]
            return carry

        lax.fori_loop(0, BX, rows, 0)

    for g in range(2):
        loads[g].wait()
        first_edges(g)
    pl.semaphore_wait(barrier, 4)
    for g in range(2):
        send(g, 0)
    lax.fori_loop(0, BX, slope_rows, 0)
    for t in range(ITERS):
        for g in range(2):
            arrive(g, t)
            sweep(g, t)
            if t + 1 < ITERS:
                send(g, t + 1)
    for t in range(ITERS):
        for g in range(2):
            left(g, t)


def sweep_grids(flux_mix, valve_adj, valve_vel, valve_src, bg_adj, bg_vel, bg_src, bg_blank):
    whole = pl.BlockSpec(memory_space=pltpu.VMEM)
    far = pl.BlockSpec(memory_space=pl.ANY)
    out = jax.ShapeDtypeStruct(valve_adj.shape, f32)
    edges = pltpu.VMEM((2, ITERS, 2, NVAR, BX, 1, BZ), f32)
    return pl.pallas_call(
        sweep_kernel,
        out_shape=(out, out),
        in_specs=[pl.BlockSpec(memory_space=pltpu.SMEM), far, whole, whole, far, whole, whole, whole],
        out_specs=(whole, whole),
        scratch_shapes=[pltpu.VMEM((NVAR, BX + 2, BY, BZ), f32)] * (2 * ITERS)
        + [
            pltpu.VMEM((2, 3, BX, BY, BZ), f32),
            pltpu.VMEM((BX, BY, BZ), f32),
            edges,
            edges,
            pltpu.SemaphoreType.DMA((2,)),
            pltpu.SemaphoreType.DMA((2, ITERS, 2, 2)),
            pltpu.SemaphoreType.DMA((2, ITERS, 2, 2)),
        ],
        compiler_params=pltpu.CompilerParams(
            collective_id=0, has_side_effects=True, vmem_limit_bytes=56 * 2**20
        ),
    )(flux_mix, valve_adj, valve_vel, valve_src, bg_adj, bg_vel, bg_src, bg_blank)


def split(x):
    hi = x.astype(bf16)
    return hi, (x - hi.astype(f32)).astype(bf16)


def as_bf16(x):
    return x.astype(f32).astype(bf16)


def pick_kernel(count_ref, cell_ref, field_ref, out_ref, table):
    for c in range(NVAR):
        hi, lo = split(field_ref[c].T)
        table[pl.ds(c * BZ, BZ), 0:PLANES] = hi
        table[pl.ds(c * BZ, BZ), PLANES : 2 * PLANES] = lo
    plane_row = as_bf16(lax.broadcasted_iota(jnp.int32, (PLANES, CAP), 0))
    depth_row = lax.broadcasted_iota(jnp.int32, (BZ, CAP), 0)
    slot = lax.broadcasted_iota(jnp.int32, (1, CAP), 1)
    one, zero = jnp.ones((), bf16), jnp.zeros((), bf16)

    def body(block, carry):
        hits, depths = [], []
        for u in range(GROUP):
            owner = block * GROUP + u
            cell = cell_ref[owner]
            hits.append(jnp.where(plane_row == as_bf16(cell >> 7), one, zero))
            depths.append(jnp.where(slot < count_ref[0, owner], cell & (BZ - 1), -1))
        hits = jnp.concatenate(hits, axis=1)
        columns = lax.dot_general(
            table[...], jnp.concatenate([hits, hits], axis=0), NN, preferred_element_type=f32
        )
        for u in range(GROUP):
            here = depth_row == depths[u]
            rows = [
                jnp.sum(
                    jnp.where(here, columns[c * BZ : (c + 1) * BZ, u * CAP : (u + 1) * CAP], 0.0),
                    axis=0,
                    keepdims=True,
                )
                for c in range(NVAR)
            ]
            out_ref[block * GROUP + u] = jnp.concatenate(rows + [jnp.zeros((3, CAP), f32)], axis=0)
        return carry

    lax.fori_loop(0, out_ref.shape[0] // GROUP, body, 0)


def pick(field, cells, counts):
    owners = cells.shape[0]
    return pl.pallas_call(
        pick_kernel,
        out_shape=jax.ShapeDtypeStruct((owners, 8, CAP), f32),
        in_specs=[
            pl.BlockSpec(memory_space=pltpu.SMEM),
            pl.BlockSpec(memory_space=pltpu.VMEM),
            pl.BlockSpec(memory_space=pltpu.VMEM),
        ],
        out_specs=pl.BlockSpec(memory_space=pltpu.VMEM),
        scratch_shapes=[pltpu.VMEM((NVAR * BZ, 2 * PLANES), bf16)],
        compiler_params=pltpu.CompilerParams(vmem_limit_bytes=56 * 2**20),
    )(counts, cells.reshape(owners, 1, CAP), field.reshape(NVAR, PLANES, BZ))


def push_kernel(value_ref, weight_ref, base_ref, field_ref, out_ref, total):
    total[...] = jnp.zeros_like(total)
    plane_row = as_bf16(lax.broadcasted_iota(jnp.int32, (PLANES, CAP), 0))
    depth_row = as_bf16(lax.broadcasted_iota(jnp.int32, (BZ, CAP), 0))
    zero = jnp.zeros((), bf16)

    def terms(sender):
        base = base_ref[sender]
        plane = base >> 7
        weight_hi, weight_lo = split(weight_ref[sender])
        value_hi, value_lo = split(value_ref[sender])
        hits = [plane_row == as_bf16(plane + off) for off in (0, 1, BY, BY + 1)]

        def spread(weight):
            halves = []
            for step in range(2):
                rows = jnp.zeros((PLANES, CAP), bf16)
                for pair in range(4):
                    rows = jnp.where(hits[pair], weight[2 * pair + step : 2 * pair + step + 1], rows)
                halves.append(rows)
            return jnp.concatenate(halves, axis=0)

        here = depth_row == as_bf16(base & (BZ - 1))

        def placed(value):
            return jnp.concatenate(
                [jnp.where(here, value[c : c + 1], zero) for c in range(NVAR)], axis=0
            )

        return spread(weight_hi), spread(weight_lo), placed(value_hi), placed(value_lo)

    def body(block, carry):
        parts = [terms(block * GROUP + u) for u in range(GROUP)]
        spread_hi, spread_lo, placed_hi, placed_lo = [[part[i] for part in parts] for i in range(4)]
        spread = jnp.concatenate(spread_hi + spread_hi + spread_lo, axis=1)
        placed = jnp.concatenate(placed_hi + placed_lo + placed_hi, axis=1)
        total[...] += lax.dot_general(placed, spread, NT, preferred_element_type=f32)
        return carry

    lax.fori_loop(0, base_ref.shape[0] // GROUP, body, 0)
    for c in range(NVAR):
        lower = total[pl.ds(c * BZ, BZ), 0:PLANES]
        upper = total[pl.ds(c * BZ, BZ), PLANES : 2 * PLANES]
        out_ref[c] = field_ref[c] + (lower + pltpu.roll(upper, 1, axis=0)).T


def push(values, weights, base, field):
    return pl.pallas_call(
        push_kernel,
        out_shape=jax.ShapeDtypeStruct((NVAR, PLANES, BZ), f32),
        in_specs=[pl.BlockSpec(memory_space=pltpu.VMEM)] * 4,
        out_specs=pl.BlockSpec(memory_space=pltpu.VMEM),
        scratch_shapes=[pltpu.VMEM((NVAR * BZ, 2 * PLANES), f32)],
        compiler_params=pltpu.CompilerParams(vmem_limit_bytes=56 * 2**20),
    )(values, weights, base, field.reshape(NVAR, PLANES, BZ))


def exchange(x):
    return lax.all_to_all(x, ("bulk", "valve"), split_axis=0, concat_axis=0, tiled=True)


def body(
    bg_adjoint,
    bg_velocity,
    bg_source,
    bg_iblank,
    valve_adjoint,
    valve_velocity,
    valve_source,
    flux_mix,
    rec_cell,
    donor_base,
    donor_weight,
    slot_count,
):
    weights = exchange(donor_weight[:, 0].transpose(1, 0, 2))
    base = exchange(donor_base[0][:, None, :])
    valve_out, bg_swept = sweep_grids(
        flux_mix, valve_adjoint, valve_velocity, valve_source, bg_adjoint, bg_velocity, bg_source, bg_iblank
    )
    values = exchange(pick(valve_out, rec_cell[0], slot_count))
    bg_out = push(values, weights, base, bg_swept).reshape(bg_adjoint.shape)
    return (bg_out, valve_out)


def solution(mesh):
    placed = (
        P(None, "bulk", "valve", None),
        P(None, "bulk", "valve", None),
        P(None, "bulk", "valve", None),
        P("bulk", "valve", None),
        P(None, "valve", "bulk", None),
        P(None, "valve", "bulk", None),
        P(None, "valve", "bulk", None),
        P(),
        P(("bulk", "valve"), None, None),
        P(("bulk", "valve"), None, None),
        P(None, ("bulk", "valve"), None, None),
        P(("bulk", "valve"), None),
    )
    return jax.shard_map(
        body,
        mesh=mesh,
        in_specs=placed,
        out_specs=(P(None, "bulk", "valve", None), P(None, "valve", "bulk", None)),
        check_vma=False,
    )
```

```python
import functools

import jax
import jax.numpy as jnp
from jax import lax
from jax.experimental import pallas as pl
from jax.experimental.pallas import tpu as pltpu
from jax.sharding import PartitionSpec as P

NVAR = 5
ITERS = 4
CAP = 128
BX = 8
BY = 32
BZ = 128
PLANES = BX * BY
PAIRS = BZ // 2

f32 = jnp.float32
bf16 = jnp.bfloat16
NT = (((1,), (1,)), ((), ()))
NN = (((1,), (0,)), ((), ()))
MESH = pl.DeviceIdType.MESH


def greet_all(bulk, valve):
    n_bulk, n_valve = lax.axis_size("bulk"), lax.axis_size("valve")
    owners = n_bulk * n_valve
    me = bulk * n_valve + valve

    def greet(step, carry):
        other = lax.rem(me + step, owners)
        pl.semaphore_signal(
            pltpu.get_barrier_semaphore(),
            inc=1,
            device_id=(other // n_valve, lax.rem(other, n_valve)),
            device_id_type=MESH,
        )
        return carry

    lax.fori_loop(1, owners, greet, 0)


def sweep_kernel(*refs):
    (flux_ref, valve_adj, valve_vel, valve_src, bg_adj, bg_vel, bg_src, bg_blank) = refs[:8]
    (weight_ref, base_ref, valve_out, bg_out, donors_in) = refs[8:13]
    fields = (refs[13 : 13 + ITERS], refs[13 + ITERS : 13 + 2 * ITERS])
    (slopes, scale, edge_in, edge_out, donors_out, load_sem, send_sem, recv_sem, away_sem, home_sem, own_sem) = refs[
        13 + 2 * ITERS :
    ]
    bulk, valve = lax.axis_index("bulk"), lax.axis_index("valve")
    n_bulk, n_valve = lax.axis_size("bulk"), lax.axis_size("valve")
    place = {"bulk": (bulk, n_bulk), "valve": (valve, n_valve)}
    axes = (("valve", "bulk"), ("bulk", "valve"))
    inputs = ((valve_adj, valve_vel, valve_src), (bg_adj, bg_vel, bg_src))
    outputs = (valve_out, bg_out)

    loads = [
        pltpu.make_async_copy(inputs[g][0], fields[g][0].at[:, pl.ds(1, BX)], load_sem.at[g])
        for g in range(2)
    ]
    for load in loads:
        load.start()

    def clear(g, side):
        index, count = place[axes[g][0]]

        @pl.when(index == (0 if side == 0 else count - 1))
        def _():
            for t in range(ITERS):
                fields[g][t][:, (BX + 1) * side] = jnp.zeros((NVAR, BY, BZ), f32)

        index, count = place[axes[g][1]]

        @pl.when(index == (0 if side == 0 else count - 1))
        def _():
            for t in range(ITERS):
                edge_in[g, t, side] = jnp.zeros((NVAR, BX, 1, BZ), f32)

    for g in range(2):
        for side in range(2):
            clear(g, side)

    greet_all(bulk, valve)

    def slope_rows(x, carry):
        for g in range(2):
            parts = [inputs[g][1][d, x] for d in range(3)]
            square = parts[0] * parts[0] + parts[1] * parts[1] + parts[2] * parts[2]
            half = 0.5 * lax.rsqrt(1.0 + square)
            for d in range(3):
                slopes[g, d, x] = parts[d] * half
        scale[x] = bg_blank[x].astype(f32) * (1.0 / 12.0)
        return carry

    def copies(g, t, side):
        away = 1 - side
        found = []
        for kind in range(2):
            index, count = place[axes[g][kind]]
            target = lax.rem(index + (1 if side else count - 1), count)
            if kind == 0:
                source = fields[g][t].at[:, BX if side else 1]
                landing = fields[g][t].at[:, 0 if side else BX + 1]
            else:
                source = edge_out.at[g, t, side]
                landing = edge_in.at[g, t, away]
            found.append(
                (
                    index < count - 1 if side else index > 0,
                    index > 0 if side else index < count - 1,
                    pltpu.make_async_remote_copy(
                        src_ref=source,
                        dst_ref=landing,
                        send_sem=send_sem.at[g, t, side, kind],
                        recv_sem=recv_sem.at[g, t, side, kind],
                        device_id={axes[g][kind]: target},
                        device_id_type=MESH,
                    ),
                )
            )
        return found

    def send(g, t):
        for side in range(2):
            for sends, _, copy in copies(g, t, side):
                pl.when(sends)(copy.start)

    def arrive(g, t):
        for side in range(2):
            for _, receives, copy in copies(g, t, side):
                pl.when(receives)(copy.wait_recv)

    def left(g, t):
        for side in range(2):
            for sends, _, copy in copies(g, t, side):
                pl.when(sends)(copy.wait_send)

    row = lax.broadcasted_iota(jnp.int32, (BY, BZ), 0)
    lane = lax.broadcasted_iota(jnp.int32, (BY, BZ), 1)

    def sweep(g, t):
        now = fields[g][t]
        source = inputs[g][2]

        def rows(x, carry):
            around, steep = [], [[], [], []]
            for c in range(NVAR):
                here = now[c, x + 1]
                x_low, x_high = now[c, x], now[c, x + 2]
                y_low = jnp.where(row == 0, edge_in[g, t, 0, c, x], pltpu.roll(here, 1, axis=0))
                y_high = jnp.where(row == BY - 1, edge_in[g, t, 1, c, x], pltpu.roll(here, BY - 1, axis=0))
                z_low = jnp.where(lane == 0, 0.0, pltpu.roll(here, 1, axis=1))
                z_high = jnp.where(lane == BZ - 1, 0.0, pltpu.roll(here, BZ - 1, axis=1))
                around.append(
                    (x_low + x_high) + (y_low + y_high) + (z_low + z_high) + source[c, x]
                )
                for d, (low, high) in enumerate(((x_low, x_high), (y_low, y_high), (z_low, z_high))):
                    steep[d].append(slopes[g, d, x] * (low - high))
            factor = scale[x] if g else 1.0 / 12.0
            for i in range(NVAR):
                total = around[i]
                for d in range(3):
                    for j in range(NVAR):
                        total = total - flux_ref[d, j, i] * steep[d][j]
                total = total * factor
                if t == ITERS - 1:
                    outputs[g][i, x] = total
                else:
                    fields[g][t + 1][i, x + 1] = total
                    edge_out[g, t + 1, 0, i, x] = total[0:1]
                    edge_out[g, t + 1, 1, i, x] = total[BY - 1 : BY]
            return carry

        lax.fori_loop(0, BX, rows, 0)

    def first_edges(g):
        def rows(x, carry):
            for c in range(NVAR):
                here = fields[g][0][c, x + 1]
                edge_out[g, 0, 0, c, x] = here[0:1]
                edge_out[g, 0, 1, c, x] = here[BY - 1 : BY]
            return carry

        lax.fori_loop(0, BX, rows, 0)

    owners = n_bulk * n_valve
    for k in range(7):
        donors_out[pl.ds(k, owners, stride=8), :] = weight_ref[k]
    donors_out[pl.ds(7, owners, stride=8), :] = base_ref[...].astype(f32)
    me = bulk * n_valve + valve

    def donor_copy(owner, landing):
        return pltpu.make_async_remote_copy(
            src_ref=donors_out.at[pl.ds(pl.multiple_of(owner * 8, 8), 8)],
            dst_ref=donors_in.at[landing],
            send_sem=away_sem.at[owner],
            recv_sem=home_sem.at[landing],
            device_id=(owner // n_valve, lax.rem(owner, n_valve)),
            device_id_type=MESH,
        )

    def send_donors(part):
        first = lax.rem(bulk + part, n_bulk) * n_valve

        def one(v, carry):
            owner = first + lax.rem(valve + v, n_valve)
            pl.when(owner != me)(donor_copy(owner, me).start)
            return carry

        lax.fori_loop(0, n_valve, one, 0)

    own = pltpu.make_async_copy(
        donors_out.at[pl.ds(pl.multiple_of(me * 8, 8), 8)], donors_in.at[me], own_sem
    )
    own.start()
    for g in range(2):
        loads[g].wait()
        first_edges(g)
    lax.fori_loop(0, BX, slope_rows, 0)
    pl.semaphore_wait(pltpu.get_barrier_semaphore(), owners - 1)
    for g in range(2):
        send(g, 0)
    part = 0
    for t in range(ITERS):
        for g in range(2):
            while part * 2 * ITERS < n_bulk * (t * 2 + g + 1):
                send_donors(part)
                part += 1
            arrive(g, t)
            sweep(g, t)
            if t + 1 < ITERS:
                send(g, t + 1)
    own.wait()

    def settle(owner, carry):
        pl.when(owner != me)(donor_copy(owner, owner).wait)
        return carry

    lax.fori_loop(0, owners, settle, 0)
    for t in range(ITERS):
        for g in range(2):
            left(g, t)


def sweep_grids(flux_mix, valve_adj, valve_vel, valve_src, bg_adj, bg_vel, bg_src, bg_blank, weights, base):
    whole = pl.BlockSpec(memory_space=pltpu.VMEM)
    far = pl.BlockSpec(memory_space=pl.ANY)
    owners = base.shape[0]
    out = jax.ShapeDtypeStruct(valve_adj.shape, f32)
    edges = pltpu.VMEM((2, ITERS, 2, NVAR, BX, 1, BZ), f32)
    return pl.pallas_call(
        sweep_kernel,
        out_shape=(out, out, jax.ShapeDtypeStruct((owners, 8, CAP), f32)),
        in_specs=[pl.BlockSpec(memory_space=pltpu.SMEM), far, whole, whole, far, whole, whole, whole, whole, whole],
        out_specs=(whole, whole, far),
        scratch_shapes=[pltpu.VMEM((NVAR, BX + 2, BY, BZ), f32)] * (2 * ITERS)
        + [
            pltpu.VMEM((2, 3, BX, BY, BZ), f32),
            pltpu.VMEM((BX, BY, BZ), f32),
            edges,
            edges,
            pltpu.VMEM((owners * 8, CAP), f32),
            pltpu.SemaphoreType.DMA((2,)),
            pltpu.SemaphoreType.DMA((2, ITERS, 2, 2)),
            pltpu.SemaphoreType.DMA((2, ITERS, 2, 2)),
            pltpu.SemaphoreType.DMA((owners,)),
            pltpu.SemaphoreType.DMA((owners,)),
            pltpu.SemaphoreType.DMA,
        ],
        compiler_params=pltpu.CompilerParams(
            collective_id=0, has_side_effects=True, vmem_limit_bytes=56 * 2**20
        ),
    )(flux_mix, valve_adj, valve_vel, valve_src, bg_adj, bg_vel, bg_src, bg_blank, weights, base)


def split(x):
    hi = x.astype(bf16)
    return hi, (x - hi.astype(f32)).astype(bf16)


def as_bf16(x):
    return x.astype(f32).astype(bf16)


def donor_kernel(
    count_ref, cell_ref, field_ref, donor_ref, swept_ref, out_ref, table, picked, arrived, total, mixed, away_sem, home_sem
):
    bulk, valve = lax.axis_index("bulk"), lax.axis_index("valve")
    n_bulk, n_valve = lax.axis_size("bulk"), lax.axis_size("valve")
    owners = n_bulk * n_valve
    me = bulk * n_valve + valve
    greet_all(bulk, valve)

    for c in range(NVAR):
        hi, lo = split(field_ref[c].T)
        table[pl.ds(c * BZ, BZ), 0:PLANES] = hi
        table[pl.ds(c * BZ, BZ), PLANES : 2 * PLANES] = lo
    total[...] = jnp.zeros_like(total)
    plane_row = as_bf16(lax.broadcasted_iota(jnp.int32, (PLANES, CAP), 0))
    depth_row = lax.broadcasted_iota(jnp.int32, (BZ, CAP), 0)
    pair_row = as_bf16(lax.broadcasted_iota(jnp.int32, (PAIRS, CAP), 0))
    slot = lax.broadcasted_iota(jnp.int32, (1, CAP), 1)
    one, zero = jnp.ones((), bf16), jnp.zeros((), bf16)

    def value_copy(owner, landing):
        return pltpu.make_async_remote_copy(
            src_ref=picked.at[owner],
            dst_ref=arrived.at[landing],
            send_sem=away_sem.at[owner],
            recv_sem=home_sem.at[landing],
            device_id=(owner // n_valve, lax.rem(owner, n_valve)),
            device_id_type=MESH,
        )

    def pick(part, carry):
        first = lax.rem(bulk + part, n_bulk) * n_valve
        hits, depths = [], []
        for u in range(n_valve):
            cell = cell_ref[first + u]
            hits.append(jnp.where(plane_row == as_bf16(cell >> 7), one, zero))
            depths.append(jnp.where(slot < count_ref[0, first + u], cell & (BZ - 1), -1))
        hits = jnp.concatenate(hits, axis=1)
        columns = lax.dot_general(
            table[...], jnp.concatenate([hits, hits], axis=0), NN, preferred_element_type=f32
        )
        for u in range(n_valve):
            here = depth_row == depths[u]
            rows = [
                jnp.sum(
                    jnp.where(here, columns[c * BZ : (c + 1) * BZ, u * CAP : (u + 1) * CAP], 0.0),
                    axis=0,
                    keepdims=True,
                )
                for c in range(NVAR)
            ]
            picked[first + u] = jnp.concatenate(rows, axis=0)

        @pl.when(part == 0)
        def _():
            pl.semaphore_wait(pltpu.get_barrier_semaphore(), owners - 1)
            arrived[me] = picked[me]

        def send(v, carry):
            owner = first + lax.rem(valve + v, n_valve)
            pl.when(owner != me)(value_copy(owner, me).start)
            return carry

        return lax.fori_loop(0, n_valve, send, carry)

    lax.fori_loop(0, n_bulk, pick, 0)

    def terms(sender):
        base = donor_ref[sender, 7:8].astype(jnp.int32)
        plane = base >> 7
        odd = (base & 1) == 1
        weight = [donor_ref[sender, k : k + 1] for k in range(7)]
        weight.append(1.0 - ((weight[0] + weight[1]) + (weight[2] + weight[3]) + (weight[4] + weight[5]) + weight[6]))
        rows = []
        for pair in range(4):
            near, deep = weight[2 * pair], weight[2 * pair + 1]
            rows += [jnp.where(odd, 0.0, near), jnp.where(odd, near, deep), jnp.where(odd, deep, 0.0)]
        weight_hi, weight_lo = split(jnp.concatenate(rows, axis=0))
        value_hi, value_lo = split(arrived[sender])
        hits = [plane_row == as_bf16(plane + off) for off in (0, 1, BY, BY + 1)]

        def spread(weight):
            thirds = []
            for step in range(3):
                rows = jnp.zeros((PLANES, CAP), bf16)
                for pair in range(4):
                    rows = jnp.where(hits[pair], weight[3 * pair + step : 3 * pair + step + 1], rows)
                thirds.append(rows)
            return jnp.concatenate(thirds, axis=0)

        here = pair_row == as_bf16((base & (BZ - 1)) >> 1)

        def placed(value):
            return jnp.concatenate(
                [jnp.where(here, value[c : c + 1], zero) for c in range(NVAR)], axis=0
            )

        return spread(weight_hi), spread(weight_lo), placed(value_hi), placed(value_lo)

    def push(part, carry):
        first = lax.rem(bulk - part + n_bulk, n_bulk) * n_valve

        def land(v, carry):
            sender = first + v
            pl.when(sender != me)(value_copy(sender, sender).wait_recv)
            return carry

        lax.fori_loop(0, n_valve, land, 0)
        parts = [terms(first + u) for u in range(n_valve)]
        spread_hi, spread_lo, placed_hi, placed_lo = [
            jnp.concatenate([part[i] for part in parts], axis=1) for i in range(4)
        ]
        both = lax.dot_general(
            jnp.concatenate([placed_hi, placed_lo], axis=0), spread_hi, NT, preferred_element_type=f32
        )
        low = lax.dot_general(placed_hi, spread_lo, NT, preferred_element_type=f32)
        total[...] += both[: NVAR * PAIRS] + both[NVAR * PAIRS :] + low
        return carry

    lax.fori_loop(0, n_bulk, push, 0)
    for c in range(NVAR):
        rows = pl.ds(c * PAIRS, PAIRS)
        even = total[rows, 0:PLANES] + pltpu.roll(total[rows, 2 * PLANES : 3 * PLANES], 1, axis=0)
        odd = total[rows, PLANES : 2 * PLANES]
        for half in range(PLANES // BZ):
            columns = slice(half * BZ, (half + 1) * BZ)
            mixed[half, pl.ds(0, PAIRS, stride=2), :] = even[:, columns]
            mixed[half, pl.ds(1, PAIRS, stride=2), :] = odd[:, columns]
            out_ref[c, pl.ds(half * BZ, BZ), :] = swept_ref[c, pl.ds(half * BZ, BZ), :] + mixed[half].T

    def left(owner, carry):
        pl.when(owner != me)(value_copy(owner, me).wait_send)
        return carry

    lax.fori_loop(0, owners, left, 0)


def donor_terms(field, cells, counts, donors, swept):
    owners = cells.shape[0]
    whole = pl.BlockSpec(memory_space=pltpu.VMEM)
    return pl.pallas_call(
        donor_kernel,
        out_shape=jax.ShapeDtypeStruct((NVAR, PLANES, BZ), f32),
        in_specs=[pl.BlockSpec(memory_space=pltpu.SMEM)] + [whole] * 4,
        out_specs=whole,
        scratch_shapes=[
            pltpu.VMEM((NVAR * BZ, 2 * PLANES), bf16),
            pltpu.VMEM((owners, NVAR, CAP), f32),
            pltpu.VMEM((owners, NVAR, CAP), f32),
            pltpu.VMEM((NVAR * PAIRS, 3 * PLANES), f32),
            pltpu.VMEM((PLANES // BZ, BZ, BZ), f32),
            pltpu.SemaphoreType.DMA((owners,)),
            pltpu.SemaphoreType.DMA((owners,)),
        ],
        compiler_params=pltpu.CompilerParams(
            collective_id=1, has_side_effects=True, vmem_limit_bytes=56 * 2**20
        ),
    )(
        counts,
        cells.reshape(owners, 1, CAP),
        field.reshape(NVAR, PLANES, BZ),
        donors,
        swept.reshape(NVAR, PLANES, BZ),
    )


def body(
    bg_adjoint,
    bg_velocity,
    bg_source,
    bg_iblank,
    valve_adjoint,
    valve_velocity,
    valve_source,
    flux_mix,
    rec_cell,
    donor_base,
    donor_weight,
    slot_count,
):
    valve_out, bg_swept, donors = sweep_grids(
        flux_mix,
        valve_adjoint,
        valve_velocity,
        valve_source,
        bg_adjoint,
        bg_velocity,
        bg_source,
        bg_iblank,
        donor_weight[:, 0],
        donor_base[0],
    )
    bg_out = donor_terms(valve_out, rec_cell[0], slot_count, donors, bg_swept).reshape(bg_adjoint.shape)
    return (bg_out, valve_out)


def solution(mesh):
    placed = (
        P(None, "bulk", "valve", None),
        P(None, "bulk", "valve", None),
        P(None, "bulk", "valve", None),
        P("bulk", "valve", None),
        P(None, "valve", "bulk", None),
        P(None, "valve", "bulk", None),
        P(None, "valve", "bulk", None),
        P(),
        P(("bulk", "valve"), None, None),
        P(("bulk", "valve"), None, None),
        P(None, ("bulk", "valve"), None, None),
        P(("bulk", "valve"), None),
    )
    return jax.shard_map(
        body,
        mesh=mesh,
        in_specs=placed,
        out_specs=(P(None, "bulk", "valve", None), P(None, "valve", "bulk", None)),
        check_vma=False,
    )
```

```python
import functools

import jax
import jax.numpy as jnp
from jax import lax
from jax.experimental import pallas as pl
from jax.experimental.pallas import tpu as pltpu
from jax.sharding import PartitionSpec as P

NVAR = 5
ITERS = 4
CAP = 128
BX = 8
BY = 32
BZ = 128
PLANES = BX * BY
PAIRS = BZ // 2
ROWS = 2

f32 = jnp.float32
bf16 = jnp.bfloat16
NT = (((1,), (1,)), ((), ()))
NN = (((1,), (0,)), ((), ()))
MESH = pl.DeviceIdType.MESH


def greet(bulk, valve):
    n_bulk, n_valve = lax.axis_size("bulk"), lax.axis_size("valve")
    barrier = pltpu.get_barrier_semaphore()
    for step in range(1, n_bulk):
        other = (lax.rem(bulk + step, n_bulk), valve)
        pl.semaphore_signal(barrier, inc=1, device_id=other, device_id_type=MESH)
    for step in range(1, n_valve):
        other = (bulk, lax.rem(valve + step, n_valve))
        pl.semaphore_signal(barrier, inc=1, device_id=other, device_id_type=MESH)


def greeted():
    pl.semaphore_wait(pltpu.get_barrier_semaphore(), lax.axis_size("bulk") + lax.axis_size("valve") - 2)


class Exchange:
    def __init__(self, source, middle, block, landed, sems):
        self.bulk, self.valve = lax.axis_index("bulk"), lax.axis_index("valve")
        self.n_bulk, self.n_valve = lax.axis_size("bulk"), lax.axis_size("valve")
        self.source, self.middle, self.block, self.landed = source, middle, block, landed
        self.sems = sems

    def first(self, v, landing):
        return pltpu.make_async_remote_copy(
            src_ref=self.source(v),
            dst_ref=self.middle.at[landing],
            send_sem=self.sems[0].at[v],
            recv_sem=self.sems[1].at[landing],
            device_id=(self.bulk, v),
            device_id_type=MESH,
        )

    def second(self, b, landing):
        return pltpu.make_async_remote_copy(
            src_ref=self.block(b),
            dst_ref=self.landed.at[landing],
            send_sem=self.sems[2].at[b],
            recv_sem=self.sems[3].at[landing],
            device_id=(b, self.valve),
            device_id_type=MESH,
        )

    def start_first(self, step):
        self.first(lax.rem(self.valve + step, self.n_valve), self.valve).start()

    def finish_first(self):
        for step in range(1, self.n_valve):
            v = lax.rem(self.valve + step, self.n_valve)
            self.first(v, v).wait_recv()

    def start_second(self):
        for step in range(1, self.n_bulk):
            self.second(lax.rem(self.bulk + step, self.n_bulk), self.bulk).start()

    def finish_second(self, b):
        self.second(b, b).wait_recv()

    def sent(self):
        for step in range(1, self.n_valve):
            v = lax.rem(self.valve + step, self.n_valve)
            self.first(v, v).wait_send()
        for step in range(1, self.n_bulk):
            b = lax.rem(self.bulk + step, self.n_bulk)
            self.second(b, b).wait_send()


def exchange_sems(n_bulk, n_valve):
    return [
        pltpu.SemaphoreType.DMA((n_valve,)),
        pltpu.SemaphoreType.DMA((n_valve,)),
        pltpu.SemaphoreType.DMA((n_bulk,)),
        pltpu.SemaphoreType.DMA((n_bulk,)),
    ]


def sweep_kernel(*refs):
    (flux_ref, valve_adj, valve_vel, valve_src, bg_adj, bg_vel, bg_src, bg_blank) = refs[:8]
    (weight_ref, base_ref, valve_out, bg_out, donors_in) = refs[8:13]
    fields = (refs[13 : 13 + ITERS], refs[13 + ITERS : 13 + 2 * ITERS])
    (slopes, scale, edge_in, edge_out, mix, donors_out, donors_mid, load_sem, send_sem, recv_sem, own_sem) = refs[
        13 + 2 * ITERS : 24 + 2 * ITERS
    ]
    donor_sems = refs[24 + 2 * ITERS :]
    bulk, valve = lax.axis_index("bulk"), lax.axis_index("valve")
    n_bulk, n_valve = lax.axis_size("bulk"), lax.axis_size("valve")
    place = {"bulk": (bulk, n_bulk), "valve": (valve, n_valve)}
    axes = (("valve", "bulk"), ("bulk", "valve"))
    inputs = ((valve_adj, valve_vel, valve_src), (bg_adj, bg_vel, bg_src))
    outputs = (valve_out, bg_out)

    loads = [
        pltpu.make_async_copy(inputs[g][0], fields[g][0].at[:, pl.ds(1, BX)], load_sem.at[g])
        for g in range(2)
    ]
    for load in loads:
        load.start()

    def clear(g, side):
        index, count = place[axes[g][0]]

        @pl.when(index == (0 if side == 0 else count - 1))
        def _():
            for t in range(ITERS):
                fields[g][t][:, (BX + 1) * side] = jnp.zeros((NVAR, BY, BZ), f32)

        index, count = place[axes[g][1]]

        @pl.when(index == (0 if side == 0 else count - 1))
        def _():
            for t in range(ITERS):
                edge_in[g, t, side] = jnp.zeros((NVAR, BX, 1, BZ), f32)

    for g in range(2):
        for side in range(2):
            clear(g, side)

    greet(bulk, valve)

    def slope_rows(x, carry):
        for g in range(2):
            parts = [inputs[g][1][d, x] for d in range(3)]
            square = parts[0] * parts[0] + parts[1] * parts[1] + parts[2] * parts[2]
            half = 0.5 * lax.rsqrt(1.0 + square)
            for d in range(3):
                slopes[g, d, x] = parts[d] * half
        scale[x] = bg_blank[x].astype(f32) * (1.0 / 12.0)
        return carry

    def copies(g, t, side):
        away = 1 - side
        found = []
        for kind in range(2):
            index, count = place[axes[g][kind]]
            target = lax.rem(index + (1 if side else count - 1), count)
            if kind == 0:
                source = fields[g][t].at[:, BX if side else 1]
                landing = fields[g][t].at[:, 0 if side else BX + 1]
            else:
                source = edge_out.at[g, t, side]
                landing = edge_in.at[g, t, away]
            found.append(
                (
                    index < count - 1 if side else index > 0,
                    index > 0 if side else index < count - 1,
                    pltpu.make_async_remote_copy(
                        src_ref=source,
                        dst_ref=landing,
                        send_sem=send_sem.at[g, t, side, kind],
                        recv_sem=recv_sem.at[g, t, side, kind],
                        device_id={axes[g][kind]: target},
                        device_id_type=MESH,
                    ),
                )
            )
        return found

    def send(g, t, kind):
        for side in range(2):
            sends, _, copy = copies(g, t, side)[kind]
            pl.when(sends)(copy.start)

    def arrive(g, t):
        for side in range(2):
            for _, receives, copy in copies(g, t, side):
                pl.when(receives)(copy.wait_recv)

    def left(g, t):
        for side in range(2):
            for sends, _, copy in copies(g, t, side):
                pl.when(sends)(copy.wait_send)

    row = lax.broadcasted_iota(jnp.int32, (BY, BZ), 0)
    lane = lax.broadcasted_iota(jnp.int32, (BY, BZ), 1)

    def fold(x):
        return x.reshape(BY // 8, 8, BZ)

    def sweep(g, t):
        now = fields[g][t]
        source = inputs[g][2]

        def rows(x, carry):
            around, steep = [], [[], [], []]
            for c in range(NVAR):
                here = now[c, x + 1]
                x_low, x_high = now[c, x], now[c, x + 2]
                y_low = jnp.where(row == 0, edge_in[g, t, 0, c, x], pltpu.roll(here, 1, axis=0))
                y_high = jnp.where(row == BY - 1, edge_in[g, t, 1, c, x], pltpu.roll(here, BY - 1, axis=0))
                z_low = jnp.where(lane == 0, 0.0, pltpu.roll(here, 1, axis=1))
                z_high = jnp.where(lane == BZ - 1, 0.0, pltpu.roll(here, BZ - 1, axis=1))
                around.append(
                    fold((x_low + x_high) + (y_low + y_high) + (z_low + z_high) + source[c, x])
                )
                for d, (low, high) in enumerate(((x_low, x_high), (y_low, y_high), (z_low, z_high))):
                    steep[d].append(fold(slopes[g, d, x] * (low - high)))
            factor = scale[x] if g else 1.0 / 12.0
            for i in range(NVAR):
                total = around[i]
                for d in range(3):
                    for j in range(NVAR):
                        total = total - mix[(d * NVAR + j) * NVAR + i] * steep[d][j]
                total = total.reshape(BY, BZ) * factor
                if t == ITERS - 1:
                    outputs[g][i, x] = total
                else:
                    fields[g][t + 1][i, x + 1] = total
                    edge_out[g, t + 1, 0, i, x] = total[0:1]
                    edge_out[g, t + 1, 1, i, x] = total[BY - 1 : BY]
            return carry

        lax.fori_loop(0, 2, lambda k, carry: rows(k * (BX - 1), carry), 0, unroll=2)
        if t + 1 < ITERS:
            send(g, t + 1, 0)
        lax.fori_loop(1, BX - 1, rows, 0, unroll=2)
        if t + 1 < ITERS:
            send(g, t + 1, 1)

    def first_edges(g):
        def rows(x, carry):
            for c in range(NVAR):
                here = fields[g][0][c, x + 1]
                edge_out[g, 0, 0, c, x] = here[0:1]
                edge_out[g, 0, 1, c, x] = here[BY - 1 : BY]
            return carry

        lax.fori_loop(0, BX, rows, 0)

    for b in range(n_bulk):
        owners = pl.ds(b * n_valve, n_valve)
        for k in range(7):
            donors_out[pl.ds(b * 8 + k, n_valve, stride=n_bulk * 8), :] = weight_ref[k, owners]
        donors_out[pl.ds(b * 8 + 7, n_valve, stride=n_bulk * 8), :] = base_ref[owners].astype(f32)

    def aligned(index, size):
        return pl.ds(pl.multiple_of(index * size, size), size)

    donors = Exchange(
        lambda v: donors_out.at[aligned(v, n_bulk * 8)],
        donors_mid,
        lambda b: donors_mid.at[:, aligned(b, 8)],
        donors_in,
        donor_sems,
    )
    for g in range(2):
        loads[g].wait()
        first_edges(g)
    greeted()
    for g in range(2):
        for kind in range(2):
            send(g, 0, kind)
    for step in range(1, n_valve):
        donors.start_first(step)
    donors_mid[valve] = donors_out[aligned(valve, n_bulk * 8)]
    lax.fori_loop(0, BX, slope_rows, 0)
    for d in range(3):
        for j in range(NVAR):
            for i in range(NVAR):
                mix[(d * NVAR + j) * NVAR + i] = jnp.broadcast_to(flux_ref[d, j : j + 1, i : i + 1], (8, BZ))
    own = pltpu.make_async_copy(donors.block(bulk), donors_in.at[bulk], own_sem)
    for t in range(ITERS):
        for g in range(2):
            arrive(g, t)
            sweep(g, t)
        if t == 1:
            donors.finish_first()
            donors.start_second()
            own.start()
    own.wait()
    for step in range(1, n_bulk):
        donors.finish_second(lax.rem(bulk + step, n_bulk))
    donors.sent()
    for t in range(ITERS):
        for g in range(2):
            left(g, t)


def sweep_grids(flux_mix, valve_adj, valve_vel, valve_src, bg_adj, bg_vel, bg_src, bg_blank, weights, base):
    whole = pl.BlockSpec(memory_space=pltpu.VMEM)
    far = pl.BlockSpec(memory_space=pl.ANY)
    n_bulk, n_valve = lax.axis_size("bulk"), lax.axis_size("valve")
    out = jax.ShapeDtypeStruct(valve_adj.shape, f32)
    edges = pltpu.VMEM((2, ITERS, 2, NVAR, BX, 1, BZ), f32)
    return pl.pallas_call(
        sweep_kernel,
        out_shape=(out, out, jax.ShapeDtypeStruct((n_bulk, n_valve, 8, CAP), f32)),
        in_specs=[whole, far, whole, whole, far, whole, whole, whole, whole, whole],
        out_specs=(whole, whole, far),
        scratch_shapes=[pltpu.VMEM((NVAR, BX + 2, BY, BZ), f32)] * (2 * ITERS)
        + [
            pltpu.VMEM((2, 3, BX, BY, BZ), f32),
            pltpu.VMEM((BX, BY, BZ), f32),
            edges,
            edges,
            pltpu.VMEM((3 * NVAR * NVAR, 8, BZ), f32),
            pltpu.VMEM((n_valve * n_bulk * 8, CAP), f32),
            pltpu.VMEM((n_valve, n_bulk * 8, CAP), f32),
            pltpu.SemaphoreType.DMA((2,)),
            pltpu.SemaphoreType.DMA((2, ITERS, 2, 2)),
            pltpu.SemaphoreType.DMA((2, ITERS, 2, 2)),
            pltpu.SemaphoreType.DMA,
        ]
        + exchange_sems(n_bulk, n_valve),
        compiler_params=pltpu.CompilerParams(
            collective_id=0, has_side_effects=True, vmem_limit_bytes=56 * 2**20
        ),
    )(flux_mix, valve_adj, valve_vel, valve_src, bg_adj, bg_vel, bg_src, bg_blank, weights, base)


def split(x):
    hi = x.astype(bf16)
    return hi, (x - hi.astype(f32)).astype(bf16)


def as_bf16(x):
    return x.astype(f32).astype(bf16)


def donor_kernel(
    count_ref, cell_ref, field_ref, donor_ref, out_ref, table, picked, middle, arrived, total, mixed, *value_sems
):
    bulk, valve = lax.axis_index("bulk"), lax.axis_index("valve")
    n_bulk, n_valve = lax.axis_size("bulk"), lax.axis_size("valve")
    greet(bulk, valve)

    for c in range(NVAR):
        hi, lo = split(field_ref[c].T)
        table[pl.ds(c * BZ, BZ), 0:PLANES] = hi
        table[pl.ds(c * BZ, BZ), PLANES : 2 * PLANES] = lo
    total[...] = jnp.zeros_like(total)
    plane_row = as_bf16(lax.broadcasted_iota(jnp.int32, (PLANES, CAP), 0))
    depth_row = lax.broadcasted_iota(jnp.int32, (BZ, CAP), 0)
    pair_row = as_bf16(lax.broadcasted_iota(jnp.int32, (PAIRS, CAP), 0))
    slot = lax.broadcasted_iota(jnp.int32, (1, CAP), 1)
    one, zero = jnp.ones((), bf16), jnp.zeros((), bf16)

    values = Exchange(
        lambda v: picked.at[v], middle, lambda b: middle.at[:, b], arrived, value_sems
    )

    def pick(part, carry):
        steps = [part * ROWS + u + 1 for u in range(ROWS)]
        rows_v = [lax.rem(valve + step, n_valve) for step in steps]
        places = [(b, v) for v in rows_v for b in range(n_bulk)]
        hits, depths = [], []
        for b, v in places:
            owner = b * n_valve + v
            cell = cell_ref[owner]
            hits.append(jnp.where(plane_row == as_bf16(cell >> 7), one, zero))
            depths.append(jnp.where(slot < count_ref[0, owner], cell & (BZ - 1), -1))
        hits = jnp.concatenate(hits, axis=1)
        columns = lax.dot_general(
            table[...], jnp.concatenate([hits, hits], axis=0), NN, preferred_element_type=f32
        )
        for u, (b, v) in enumerate(places):
            here = depth_row == depths[u]
            rows = [
                jnp.sum(
                    jnp.where(here, columns[c * BZ : (c + 1) * BZ, u * CAP : (u + 1) * CAP], 0.0),
                    axis=0,
                    keepdims=True,
                )
                for c in range(NVAR)
            ]
            picked[v, b] = jnp.concatenate(rows, axis=0)
        pl.when(part == 0)(greeted)
        for step in steps:
            pl.when(step < n_valve)(lambda step=step: values.start_first(step))
        return carry

    lax.fori_loop(0, n_valve // ROWS, pick, 0)
    middle[valve] = picked[valve]
    values.finish_first()
    values.start_second()
    for v in range(n_valve):
        arrived[bulk, v] = middle[v, bulk]

    def terms(group, sender):
        base = donor_ref[group, sender, 7:8].astype(jnp.int32)
        plane = base >> 7
        odd = (base & 1) == 1
        weight = [donor_ref[group, sender, k : k + 1] for k in range(7)]
        weight.append(1.0 - ((weight[0] + weight[1]) + (weight[2] + weight[3]) + (weight[4] + weight[5]) + weight[6]))
        rows = []
        for pair in range(4):
            near, deep = weight[2 * pair], weight[2 * pair + 1]
            rows += [jnp.where(odd, 0.0, near), jnp.where(odd, near, deep), jnp.where(odd, deep, 0.0)]
        weight_hi, weight_lo = split(jnp.concatenate(rows, axis=0))
        value_hi, value_lo = split(arrived[group, sender])
        hits = [plane_row == as_bf16(plane + off) for off in (0, 1, BY, BY + 1)]

        def spread(weight):
            thirds = []
            for step in range(3):
                rows = jnp.zeros((PLANES, CAP), bf16)
                for pair in range(4):
                    rows = jnp.where(hits[pair], weight[3 * pair + step : 3 * pair + step + 1], rows)
                thirds.append(rows)
            return jnp.concatenate(thirds, axis=0)

        here = pair_row == as_bf16((base & (BZ - 1)) >> 1)

        def placed(value):
            return jnp.concatenate(
                [jnp.where(here, value[c : c + 1], zero) for c in range(NVAR)], axis=0
            )

        return spread(weight_hi), spread(weight_lo), placed(value_hi), placed(value_lo)

    def push(part, carry):
        group = lax.rem(bulk - part + n_bulk, n_bulk)
        pl.when(part > 0)(lambda: values.finish_second(group))
        parts = [terms(group, v) for v in range(n_valve)]
        spread_hi, spread_lo, placed_hi, placed_lo = [
            jnp.concatenate([part[i] for part in parts], axis=1) for i in range(4)
        ]
        both = lax.dot_general(
            jnp.concatenate([placed_hi, placed_lo], axis=0), spread_hi, NT, preferred_element_type=f32
        )
        low = lax.dot_general(placed_hi, spread_lo, NT, preferred_element_type=f32)
        total[...] += both[: NVAR * PAIRS] + both[NVAR * PAIRS :] + low
        return carry

    lax.fori_loop(0, n_bulk, push, 0)
    for c in range(NVAR):
        rows = pl.ds(c * PAIRS, PAIRS)
        even = total[rows, 0:PLANES] + pltpu.roll(total[rows, 2 * PLANES : 3 * PLANES], 1, axis=0)
        odd = total[rows, PLANES : 2 * PLANES]
        for half in range(PLANES // BZ):
            columns = slice(half * BZ, (half + 1) * BZ)
            mixed[half, pl.ds(0, PAIRS, stride=2), :] = even[:, columns]
            mixed[half, pl.ds(1, PAIRS, stride=2), :] = odd[:, columns]
            out_ref[c, pl.ds(half * BZ, BZ), :] = mixed[half].T

    values.sent()


def donor_terms(field, cells, counts, donors):
    n_bulk, n_valve, _, _ = donors.shape
    whole = pl.BlockSpec(memory_space=pltpu.VMEM)
    return pl.pallas_call(
        donor_kernel,
        out_shape=jax.ShapeDtypeStruct((NVAR, PLANES, BZ), f32),
        in_specs=[pl.BlockSpec(memory_space=pltpu.SMEM)] + [whole] * 3,
        out_specs=whole,
        scratch_shapes=[
            pltpu.VMEM((NVAR * BZ, 2 * PLANES), bf16),
            pltpu.VMEM((n_valve, n_bulk, NVAR, CAP), f32),
            pltpu.VMEM((n_valve, n_bulk, NVAR, CAP), f32),
            pltpu.VMEM((n_bulk, n_valve, NVAR, CAP), f32),
            pltpu.VMEM((NVAR * PAIRS, 3 * PLANES), f32),
            pltpu.VMEM((PLANES // BZ, BZ, BZ), f32),
        ]
        + exchange_sems(n_bulk, n_valve),
        compiler_params=pltpu.CompilerParams(
            collective_id=1, has_side_effects=True, vmem_limit_bytes=56 * 2**20
        ),
    )(counts, cells.reshape(n_bulk * n_valve, 1, CAP), field.reshape(NVAR, PLANES, BZ), donors)


def body(
    bg_adjoint,
    bg_velocity,
    bg_source,
    bg_iblank,
    valve_adjoint,
    valve_velocity,
    valve_source,
    flux_mix,
    rec_cell,
    donor_base,
    donor_weight,
    slot_count,
):
    valve_out, bg_swept, donors = sweep_grids(
        flux_mix,
        valve_adjoint,
        valve_velocity,
        valve_source,
        bg_adjoint,
        bg_velocity,
        bg_source,
        bg_iblank,
        donor_weight[:, 0],
        donor_base[0],
    )
    pushed = donor_terms(valve_out, rec_cell[0], slot_count, donors)
    bg_out = bg_swept + pushed.reshape(bg_swept.shape)
    return (bg_out, valve_out)


def solution(mesh):
    placed = (
        P(None, "bulk", "valve", None),
        P(None, "bulk", "valve", None),
        P(None, "bulk", "valve", None),
        P("bulk", "valve", None),
        P(None, "valve", "bulk", None),
        P(None, "valve", "bulk", None),
        P(None, "valve", "bulk", None),
        P(),
        P(("bulk", "valve"), None, None),
        P(("bulk", "valve"), None, None),
        P(None, ("bulk", "valve"), None, None),
        P(("bulk", "valve"), None),
    )
    return jax.shard_map(
        body,
        mesh=mesh,
        in_specs=placed,
        out_specs=(P(None, "bulk", "valve", None), P(None, "valve", "bulk", None)),
        check_vma=False,
    )
```

```python
import functools

import jax
import jax.numpy as jnp
from jax import lax
from jax.experimental import pallas as pl
from jax.experimental.pallas import tpu as pltpu
from jax.sharding import PartitionSpec as P

NVAR = 5
ITERS = 4
CAP = 128
BX = 8
BY = 32
BZ = 128
PLANES = BX * BY
PAIRS = BZ // 2
ROWS = 2

f32 = jnp.float32
bf16 = jnp.bfloat16
NT = (((1,), (1,)), ((), ()))
NN = (((1,), (0,)), ((), ()))
MESH = pl.DeviceIdType.MESH


def greet(bulk, valve):
    n_bulk, n_valve = lax.axis_size("bulk"), lax.axis_size("valve")
    barrier = pltpu.get_barrier_semaphore()
    for step in range(1, n_bulk):
        other = (lax.rem(bulk + step, n_bulk), valve)
        pl.semaphore_signal(barrier, inc=1, device_id=other, device_id_type=MESH)
    for step in range(1, n_valve):
        other = (bulk, lax.rem(valve + step, n_valve))
        pl.semaphore_signal(barrier, inc=1, device_id=other, device_id_type=MESH)


def greeted():
    pl.semaphore_wait(pltpu.get_barrier_semaphore(), lax.axis_size("bulk") + lax.axis_size("valve") - 2)


class Exchange:
    def __init__(self, source, middle, block, landed, sems):
        self.bulk, self.valve = lax.axis_index("bulk"), lax.axis_index("valve")
        self.n_bulk, self.n_valve = lax.axis_size("bulk"), lax.axis_size("valve")
        self.source, self.middle, self.block, self.landed = source, middle, block, landed
        self.sems = sems

    def first(self, v, landing):
        return pltpu.make_async_remote_copy(
            src_ref=self.source(v),
            dst_ref=self.middle.at[landing],
            send_sem=self.sems[0].at[v],
            recv_sem=self.sems[1].at[landing],
            device_id=(self.bulk, v),
            device_id_type=MESH,
        )

    def second(self, b, landing):
        return pltpu.make_async_remote_copy(
            src_ref=self.block(b),
            dst_ref=self.landed.at[landing],
            send_sem=self.sems[2].at[b],
            recv_sem=self.sems[3].at[landing],
            device_id=(b, self.valve),
            device_id_type=MESH,
        )

    def start_first(self, step):
        self.first(lax.rem(self.valve + step, self.n_valve), self.valve).start()

    def finish_first(self):
        for step in range(1, self.n_valve):
            v = lax.rem(self.valve + step, self.n_valve)
            self.first(v, v).wait_recv()

    def start_second(self):
        for step in range(1, self.n_bulk):
            self.second(lax.rem(self.bulk + step, self.n_bulk), self.bulk).start()

    def finish_second(self, b):
        self.second(b, b).wait_recv()

    def sent(self):
        for step in range(1, self.n_valve):
            v = lax.rem(self.valve + step, self.n_valve)
            self.first(v, v).wait_send()
        for step in range(1, self.n_bulk):
            b = lax.rem(self.bulk + step, self.n_bulk)
            self.second(b, b).wait_send()


def exchange_sems(n_bulk, n_valve):
    return [
        pltpu.SemaphoreType.DMA((n_valve,)),
        pltpu.SemaphoreType.DMA((n_valve,)),
        pltpu.SemaphoreType.DMA((n_bulk,)),
        pltpu.SemaphoreType.DMA((n_bulk,)),
    ]


def split(x):
    hi = x.astype(bf16)
    return hi, (x - hi.astype(f32)).astype(bf16)


def as_bf16(x):
    return x.astype(f32).astype(bf16)


def step_kernel(*refs):
    (flux_ref, count_ref, valve_adj, bg_adj) = refs[:4]
    far, (valve_out, bg_out) = refs[4:12], refs[12:14]
    fields = (refs[14 : 14 + ITERS], refs[14 + ITERS : 14 + 2 * ITERS])
    (slopes, scale, edge_in, edge_out, mix, donors_out, donors_mid, donors_in) = refs[22:30]
    (bg_swept, table, picked, middle, arrived, total, mixed) = refs[30:37]
    near = refs[37:45]
    (valve_vel, bg_vel, bg_blank, valve_src, bg_src, weight_ref, base_ref, cell_ref) = near
    (load_sem, send_sem, recv_sem) = refs[45:48]
    donor_sems, value_sems = refs[48:52], refs[52:56]
    bulk, valve = lax.axis_index("bulk"), lax.axis_index("valve")
    n_bulk, n_valve = lax.axis_size("bulk"), lax.axis_size("valve")
    place = {"bulk": (bulk, n_bulk), "valve": (valve, n_valve)}
    axes = (("valve", "bulk"), ("bulk", "valve"))
    inputs = ((valve_adj, valve_vel, valve_src), (bg_adj, bg_vel, bg_src))
    outputs = (valve_out, bg_swept)

    loads = [
        pltpu.make_async_copy(inputs[g][0], fields[g][0].at[:, pl.ds(1, BX)], load_sem.at[g])
        for g in range(2)
    ]
    loads += [pltpu.make_async_copy(far[k], near[k], load_sem.at[2 + k]) for k in range(len(near))]
    for load in loads:
        load.start()

    def clear(g, side):
        index, count = place[axes[g][0]]

        @pl.when(index == (0 if side == 0 else count - 1))
        def _():
            for t in range(ITERS):
                fields[g][t][:, (BX + 1) * side] = jnp.zeros((NVAR, BY, BZ), f32)

        index, count = place[axes[g][1]]

        @pl.when(index == (0 if side == 0 else count - 1))
        def _():
            for t in range(ITERS):
                edge_in[g, t, side] = jnp.zeros((NVAR, BX, 1, BZ), f32)

    for g in range(2):
        for side in range(2):
            clear(g, side)

    greet(bulk, valve)

    def slope_rows(x, carry):
        for g in range(2):
            parts = [inputs[g][1][d, x] for d in range(3)]
            square = parts[0] * parts[0] + parts[1] * parts[1] + parts[2] * parts[2]
            half = 0.5 * lax.rsqrt(1.0 + square)
            for d in range(3):
                slopes[g, d, x] = parts[d] * half
        scale[x] = bg_blank[x].astype(f32) * (1.0 / 12.0)
        return carry

    def copies(g, t, side):
        away = 1 - side
        found = []
        for kind in range(2):
            index, count = place[axes[g][kind]]
            target = lax.rem(index + (1 if side else count - 1), count)
            if kind == 0:
                source = fields[g][t].at[:, BX if side else 1]
                landing = fields[g][t].at[:, 0 if side else BX + 1]
            else:
                source = edge_out.at[g, t, side]
                landing = edge_in.at[g, t, away]
            found.append(
                (
                    index < count - 1 if side else index > 0,
                    index > 0 if side else index < count - 1,
                    pltpu.make_async_remote_copy(
                        src_ref=source,
                        dst_ref=landing,
                        send_sem=send_sem.at[g, t, side, kind],
                        recv_sem=recv_sem.at[g, t, side, kind],
                        device_id={axes[g][kind]: target},
                        device_id_type=MESH,
                    ),
                )
            )
        return found

    def send(g, t, kind):
        for side in range(2):
            sends, _, copy = copies(g, t, side)[kind]
            pl.when(sends)(copy.start)

    def arrive(g, t):
        for side in range(2):
            for _, receives, copy in copies(g, t, side):
                pl.when(receives)(copy.wait_recv)

    def left(g, t):
        for side in range(2):
            for sends, _, copy in copies(g, t, side):
                pl.when(sends)(copy.wait_send)

    row = lax.broadcasted_iota(jnp.int32, (BY, BZ), 0)
    lane = lax.broadcasted_iota(jnp.int32, (BY, BZ), 1)

    def fold(x):
        return x.reshape(BY // 8, 8, BZ)

    def sweep(g, t):
        now = fields[g][t]
        source = inputs[g][2]

        def rows(x, carry):
            around, steep = [], [[], [], []]
            for c in range(NVAR):
                here = now[c, x + 1]
                x_low, x_high = now[c, x], now[c, x + 2]
                y_low = jnp.where(row == 0, edge_in[g, t, 0, c, x], pltpu.roll(here, 1, axis=0))
                y_high = jnp.where(row == BY - 1, edge_in[g, t, 1, c, x], pltpu.roll(here, BY - 1, axis=0))
                z_low = jnp.where(lane == 0, 0.0, pltpu.roll(here, 1, axis=1))
                z_high = jnp.where(lane == BZ - 1, 0.0, pltpu.roll(here, BZ - 1, axis=1))
                around.append(
                    fold((x_low + x_high) + (y_low + y_high) + (z_low + z_high) + source[c, x])
                )
                for d, (low, high) in enumerate(((x_low, x_high), (y_low, y_high), (z_low, z_high))):
                    steep[d].append(fold(slopes[g, d, x] * (low - high)))
            factor = scale[x] if g else 1.0 / 12.0
            for i in range(NVAR):
                total = around[i]
                for d in range(3):
                    for j in range(NVAR):
                        total = total - mix[(d * NVAR + j) * NVAR + i] * steep[d][j]
                total = total.reshape(BY, BZ) * factor
                if t == ITERS - 1:
                    outputs[g][i, x] = total
                else:
                    fields[g][t + 1][i, x + 1] = total
                    edge_out[g, t + 1, 0, i, x] = total[0:1]
                    edge_out[g, t + 1, 1, i, x] = total[BY - 1 : BY]
            return carry

        lax.fori_loop(0, 2, lambda k, carry: rows(k * (BX - 1), carry), 0, unroll=2)
        if t + 1 < ITERS:
            send(g, t + 1, 0)
        lax.fori_loop(1, BX - 1, rows, 0, unroll=2)
        if t + 1 < ITERS:
            send(g, t + 1, 1)

    def first_edges(g):
        def rows(x, carry):
            for c in range(NVAR):
                here = fields[g][0][c, x + 1]
                edge_out[g, 0, 0, c, x] = here[0:1]
                edge_out[g, 0, 1, c, x] = here[BY - 1 : BY]
            return carry

        lax.fori_loop(0, BX, rows, 0)

    loads[7].wait()
    loads[8].wait()
    for b in range(n_bulk):
        owners = pl.ds(b * n_valve, n_valve)
        for k in range(7):
            donors_out[pl.ds(b * 8 + k, n_valve, stride=n_bulk * 8), :] = weight_ref[k, owners]
        donors_out[pl.ds(b * 8 + 7, n_valve, stride=n_bulk * 8), :] = base_ref[owners].astype(f32)

    def aligned(index, size):
        return pl.ds(pl.multiple_of(index * size, size), size)

    donors = Exchange(
        lambda v: donors_out.at[aligned(v, n_bulk * 8)],
        donors_mid,
        lambda b: donors_mid.at[:, aligned(b, 8)],
        donors_in,
        donor_sems,
    )
    for g in range(2):
        loads[g].wait()
        first_edges(g)
    greeted()
    for g in range(2):
        for kind in range(2):
            send(g, 0, kind)
    donors_mid[valve] = donors_out[aligned(valve, n_bulk * 8)]
    for k in (2, 3, 4):
        loads[k].wait()
    lax.fori_loop(0, BX, slope_rows, 0)
    for d in range(3):
        for j in range(NVAR):
            for i in range(NVAR):
                mix[(d * NVAR + j) * NVAR + i] = jnp.broadcast_to(flux_ref[j, d : d + 1, i : i + 1], (8, BZ))
    for k in (5, 6, 9):
        loads[k].wait()
    for t in range(ITERS):
        arrive(0, t)
        sweep(0, t)
        if t + 1 < ITERS:
            arrive(1, t)
            sweep(1, t)

    for step in range(1, n_valve):
        donors.start_first(step)
    for c in range(NVAR):
        hi, lo = split(valve_out[c].reshape(PLANES, BZ).T)
        table[pl.ds(c * BZ, BZ), 0:PLANES] = hi
        table[pl.ds(c * BZ, BZ), PLANES : 2 * PLANES] = lo
    total[...] = jnp.zeros_like(total)
    plane_row = as_bf16(lax.broadcasted_iota(jnp.int32, (PLANES, CAP), 0))
    depth_row = lax.broadcasted_iota(jnp.int32, (BZ, CAP), 0)
    pair_row = as_bf16(lax.broadcasted_iota(jnp.int32, (PAIRS, CAP), 0))
    slot = lax.broadcasted_iota(jnp.int32, (1, CAP), 1)
    one, zero = jnp.ones((), bf16), jnp.zeros((), bf16)

    values = Exchange(
        lambda v: picked.at[v], middle, lambda b: middle.at[:, b], arrived, value_sems
    )

    def pick(part, carry):
        steps = [part * ROWS + u + 1 for u in range(ROWS)]
        rows_v = [lax.rem(valve + step, n_valve) for step in steps]
        places = [(b, v) for v in rows_v for b in range(n_bulk)]
        hits, depths = [], []
        for b, v in places:
            owner = b * n_valve + v
            cell = cell_ref[owner]
            hits.append(jnp.where(plane_row == as_bf16(cell >> 7), one, zero))
            depths.append(jnp.where(slot < count_ref[0, owner], cell & (BZ - 1), -1))
        hits = jnp.concatenate(hits, axis=1)
        columns = lax.dot_general(
            table[...], jnp.concatenate([hits, hits], axis=0), NN, preferred_element_type=f32
        )
        for u, (b, v) in enumerate(places):
            here = depth_row == depths[u]
            rows = [
                jnp.sum(
                    jnp.where(here, columns[c * BZ : (c + 1) * BZ, u * CAP : (u + 1) * CAP], 0.0),
                    axis=0,
                    keepdims=True,
                )
                for c in range(NVAR)
            ]
            picked[v, b] = jnp.concatenate(rows, axis=0)
        for step in steps:
            pl.when(step < n_valve)(lambda step=step: values.start_first(step))
        return carry

    parts = n_valve // ROWS
    lax.fori_loop(0, parts // 2, pick, 0)
    donors.finish_first()
    donors.start_second()
    for v in range(n_valve):
        donors_in[bulk, v] = donors_mid[v, aligned(bulk, 8)]
    lax.fori_loop(parts // 2, parts, pick, 0)
    middle[valve] = picked[valve]
    arrive(1, ITERS - 1)
    sweep(1, ITERS - 1)
    values.finish_first()
    values.start_second()
    for v in range(n_valve):
        arrived[bulk, v] = middle[v, bulk]

    def terms(group, sender):
        base = donors_in[group, sender, 7:8].astype(jnp.int32)
        plane = base >> 7
        odd = (base & 1) == 1
        weight = [donors_in[group, sender, k : k + 1] for k in range(7)]
        weight.append(1.0 - ((weight[0] + weight[1]) + (weight[2] + weight[3]) + (weight[4] + weight[5]) + weight[6]))
        rows = []
        for pair in range(4):
            near, deep = weight[2 * pair], weight[2 * pair + 1]
            rows += [jnp.where(odd, 0.0, near), jnp.where(odd, near, deep), jnp.where(odd, deep, 0.0)]
        weight_hi, weight_lo = split(jnp.concatenate(rows, axis=0))
        value_hi, value_lo = split(arrived[group, sender])
        hits = [plane_row == as_bf16(plane + off) for off in (0, 1, BY, BY + 1)]

        def spread(weight):
            thirds = []
            for step in range(3):
                rows = jnp.zeros((PLANES, CAP), bf16)
                for pair in range(4):
                    rows = jnp.where(hits[pair], weight[3 * pair + step : 3 * pair + step + 1], rows)
                thirds.append(rows)
            return jnp.concatenate(thirds, axis=0)

        here = pair_row == as_bf16((base & (BZ - 1)) >> 1)

        def placed(value):
            return jnp.concatenate(
                [jnp.where(here, value[c : c + 1], zero) for c in range(NVAR)], axis=0
            )

        return spread(weight_hi), spread(weight_lo), placed(value_hi), placed(value_lo)

    def push(part, carry):
        group = lax.rem(bulk - part + n_bulk, n_bulk)

        @pl.when(part > 0)
        def _():
            donors.finish_second(group)
            values.finish_second(group)

        found = [terms(group, v) for v in range(n_valve)]
        spread_hi, spread_lo, placed_hi, placed_lo = [
            jnp.concatenate([one[i] for one in found], axis=1) for i in range(4)
        ]
        both = lax.dot_general(
            jnp.concatenate([placed_hi, placed_lo], axis=0), spread_hi, NT, preferred_element_type=f32
        )
        low = lax.dot_general(placed_hi, spread_lo, NT, preferred_element_type=f32)
        total[...] += both[: NVAR * PAIRS] + both[NVAR * PAIRS :] + low
        return carry

    lax.fori_loop(0, n_bulk, push, 0)
    for c in range(NVAR):
        rows = pl.ds(c * PAIRS, PAIRS)
        even = total[rows, 0:PLANES] + pltpu.roll(total[rows, 2 * PLANES : 3 * PLANES], 1, axis=0)
        odd = total[rows, PLANES : 2 * PLANES]
        for half in range(PLANES // BZ):
            columns = slice(half * BZ, (half + 1) * BZ)
            mixed[half, pl.ds(0, PAIRS, stride=2), :] = even[:, columns]
            mixed[half, pl.ds(1, PAIRS, stride=2), :] = odd[:, columns]
            here = pl.ds(half * (BX // 2), BX // 2)
            bg_out[c, here] = bg_swept[c, here] + mixed[half].T.reshape(BX // 2, BY, BZ)

    values.sent()
    donors.sent()
    for t in range(ITERS):
        for g in range(2):
            left(g, t)


def whole_step(flux_mix, counts, valve_adj, bg_adj, *rest):
    whole = pl.BlockSpec(memory_space=pltpu.VMEM)
    far = pl.BlockSpec(memory_space=pltpu.HBM)
    small = pl.BlockSpec(memory_space=pltpu.SMEM)
    n_bulk, n_valve = lax.axis_size("bulk"), lax.axis_size("valve")
    out = jax.ShapeDtypeStruct(valve_adj.shape, f32)
    edges = pltpu.VMEM((2, ITERS, 2, NVAR, BX, 1, BZ), f32)
    return pl.pallas_call(
        step_kernel,
        out_shape=(out, out),
        in_specs=[whole, small] + [far] * 10,
        out_specs=(whole, whole),
        scratch_shapes=[pltpu.VMEM((NVAR, BX + 2, BY, BZ), f32)] * (2 * ITERS)
        + [
            pltpu.VMEM((2, 3, BX, BY, BZ), f32),
            pltpu.VMEM((BX, BY, BZ), f32),
            edges,
            edges,
            pltpu.VMEM((3 * NVAR * NVAR, 8, BZ), f32),
            pltpu.VMEM((n_valve * n_bulk * 8, CAP), f32),
            pltpu.VMEM((n_valve, n_bulk * 8, CAP), f32),
            pltpu.VMEM((n_bulk, n_valve, 8, CAP), f32),
            pltpu.VMEM((NVAR, BX, BY, BZ), f32),
            pltpu.VMEM((NVAR * BZ, 2 * PLANES), bf16),
            pltpu.VMEM((n_valve, n_bulk, NVAR, CAP), f32),
            pltpu.VMEM((n_valve, n_bulk, NVAR, CAP), f32),
            pltpu.VMEM((n_bulk, n_valve, NVAR, CAP), f32),
            pltpu.VMEM((NVAR * PAIRS, 3 * PLANES), f32),
            pltpu.VMEM((PLANES // BZ, BZ, BZ), f32),
        ]
        + [pltpu.VMEM(x.shape, x.dtype) for x in rest]
        + [
            pltpu.SemaphoreType.DMA((2 + len(rest),)),
            pltpu.SemaphoreType.DMA((2, ITERS, 2, 2)),
            pltpu.SemaphoreType.DMA((2, ITERS, 2, 2)),
        ]
        + exchange_sems(n_bulk, n_valve) * 2,
        compiler_params=pltpu.CompilerParams(
            collective_id=0, has_side_effects=True, vmem_limit_bytes=56 * 2**20
        ),
    )(flux_mix, counts, valve_adj, bg_adj, *rest)


def body(
    bg_adjoint,
    bg_velocity,
    bg_source,
    bg_iblank,
    valve_adjoint,
    valve_velocity,
    valve_source,
    flux_mix,
    rec_cell,
    donor_base,
    donor_weight,
    slot_count,
):
    n_owners = rec_cell.shape[1]
    valve_out, bg_out = whole_step(
        flux_mix.transpose(1, 0, 2),
        slot_count,
        valve_adjoint,
        bg_adjoint,
        valve_velocity,
        bg_velocity,
        bg_iblank,
        valve_source,
        bg_source,
        donor_weight[:, 0],
        donor_base[0],
        rec_cell.reshape(n_owners, 1, CAP),
    )
    return (bg_out, valve_out)


def solution(mesh):
    placed = (
        P(None, "bulk", "valve", None),
        P(None, "bulk", "valve", None),
        P(None, "bulk", "valve", None),
        P("bulk", "valve", None),
        P(None, "valve", "bulk", None),
        P(None, "valve", "bulk", None),
        P(None, "valve", "bulk", None),
        P(),
        P(("bulk", "valve"), None, None),
        P(("bulk", "valve"), None, None),
        P(None, ("bulk", "valve"), None, None),
        P(("bulk", "valve"), None),
    )
    return jax.shard_map(
        body,
        mesh=mesh,
        in_specs=placed,
        out_specs=(P(None, "bulk", "valve", None), P(None, "valve", "bulk", None)),
        check_vma=False,
    )
```

```python
import functools

import jax
import jax.numpy as jnp
from jax import lax
from jax.experimental import pallas as pl
from jax.experimental.pallas import tpu as pltpu
from jax.sharding import PartitionSpec as P

NVAR = 5
ITERS = 4
CAP = 128
BX = 8
BY = 32
BZ = 128
PLANES = BX * BY
PAIRS = BZ // 2
ROWS = 2

f32 = jnp.float32
bf16 = jnp.bfloat16
NT = (((1,), (1,)), ((), ()))
NN = (((1,), (0,)), ((), ()))
MESH = pl.DeviceIdType.MESH


def greet(bulk, valve):
    n_bulk, n_valve = lax.axis_size("bulk"), lax.axis_size("valve")
    barrier = pltpu.get_barrier_semaphore()
    for step in range(1, n_bulk):
        other = (lax.rem(bulk + step, n_bulk), valve)
        pl.semaphore_signal(barrier, inc=1, device_id=other, device_id_type=MESH)
    for step in range(1, n_valve):
        other = (bulk, lax.rem(valve + step, n_valve))
        pl.semaphore_signal(barrier, inc=1, device_id=other, device_id_type=MESH)


def greeted():
    pl.semaphore_wait(pltpu.get_barrier_semaphore(), lax.axis_size("bulk") + lax.axis_size("valve") - 2)


class Exchange:
    def __init__(self, source, middle, block, landed, sems):
        self.bulk, self.valve = lax.axis_index("bulk"), lax.axis_index("valve")
        self.n_bulk, self.n_valve = lax.axis_size("bulk"), lax.axis_size("valve")
        self.source, self.middle, self.block, self.landed = source, middle, block, landed
        self.sems = sems

    def first(self, v, landing):
        return pltpu.make_async_remote_copy(
            src_ref=self.source(v),
            dst_ref=self.middle.at[landing],
            send_sem=self.sems[0].at[v],
            recv_sem=self.sems[1].at[landing],
            device_id=(self.bulk, v),
            device_id_type=MESH,
        )

    def second(self, b, landing):
        return pltpu.make_async_remote_copy(
            src_ref=self.block(b),
            dst_ref=self.landed.at[landing],
            send_sem=self.sems[2].at[b],
            recv_sem=self.sems[3].at[landing],
            device_id=(b, self.valve),
            device_id_type=MESH,
        )

    def start_first(self, step):
        self.first(lax.rem(self.valve + step, self.n_valve), self.valve).start()

    def finish_first(self):
        for step in range(1, self.n_valve):
            v = lax.rem(self.valve + step, self.n_valve)
            self.first(v, v).wait_recv()

    def start_second(self):
        for step in range(1, self.n_bulk):
            self.second(lax.rem(self.bulk + step, self.n_bulk), self.bulk).start()

    def finish_second(self, b):
        self.second(b, b).wait_recv()

    def sent(self):
        for step in range(1, self.n_valve):
            v = lax.rem(self.valve + step, self.n_valve)
            self.first(v, v).wait_send()
        for step in range(1, self.n_bulk):
            b = lax.rem(self.bulk + step, self.n_bulk)
            self.second(b, b).wait_send()


def exchange_sems(n_bulk, n_valve):
    return [
        pltpu.SemaphoreType.DMA((n_valve,)),
        pltpu.SemaphoreType.DMA((n_valve,)),
        pltpu.SemaphoreType.DMA((n_bulk,)),
        pltpu.SemaphoreType.DMA((n_bulk,)),
    ]


def split(x):
    hi = x.astype(bf16)
    return hi, (x - hi.astype(f32)).astype(bf16)


def as_bf16(x):
    return x.astype(f32).astype(bf16)


def step_kernel(*refs):
    (flux_ref, count_ref, valve_adj, bg_adj) = refs[:4]
    far, (valve_out, bg_out) = refs[4:12], refs[12:14]
    fields = (refs[14 : 14 + ITERS], refs[14 + ITERS : 14 + 2 * ITERS])
    (slopes, scale, edge_in, edge_out, mix, donors_out, donors_mid, donors_in) = refs[22:30]
    (bg_swept, table, picked, middle, arrived, total, mixed) = refs[30:37]
    near = refs[37:45]
    (valve_vel, bg_vel, bg_blank, valve_src, bg_src, weight_ref, base_ref, cell_ref) = near
    (load_sem, send_sem, recv_sem) = refs[45:48]
    donor_sems, value_sems = refs[48:52], refs[52:56]
    bulk, valve = lax.axis_index("bulk"), lax.axis_index("valve")
    n_bulk, n_valve = lax.axis_size("bulk"), lax.axis_size("valve")
    place = {"bulk": (bulk, n_bulk), "valve": (valve, n_valve)}
    axes = (("valve", "bulk"), ("bulk", "valve"))
    inputs = ((valve_adj, valve_vel, valve_src), (bg_adj, bg_vel, bg_src))
    outputs = (valve_out, bg_swept)

    loads = [
        pltpu.make_async_copy(inputs[g][0], fields[g][0].at[:, pl.ds(1, BX)], load_sem.at[g])
        for g in range(2)
    ]
    for load in loads:
        load.start()
    loads += [pltpu.make_async_copy(far[k], near[k], load_sem.at[2 + k]) for k in range(len(near))]

    def clear(g, side):
        index, count = place[axes[g][0]]

        @pl.when(index == (0 if side == 0 else count - 1))
        def _():
            for t in range(ITERS):
                fields[g][t][:, (BX + 1) * side] = jnp.zeros((NVAR, BY, BZ), f32)

        index, count = place[axes[g][1]]

        @pl.when(index == (0 if side == 0 else count - 1))
        def _():
            for t in range(ITERS):
                edge_in[g, t, side] = jnp.zeros((NVAR, BX, 1, BZ), f32)

    for g in range(2):
        for side in range(2):
            clear(g, side)

    greet(bulk, valve)

    def slope_rows(x, carry):
        for g in range(2):
            parts = [inputs[g][1][d, x] for d in range(3)]
            square = parts[0] * parts[0] + parts[1] * parts[1] + parts[2] * parts[2]
            half = 0.5 * lax.rsqrt(1.0 + square)
            for d in range(3):
                slopes[g, d, x] = parts[d] * half
        scale[x] = bg_blank[x].astype(f32) * (1.0 / 12.0)
        return carry

    def copies(g, t, side):
        away = 1 - side
        found = []
        for kind in range(2):
            index, count = place[axes[g][kind]]
            target = lax.rem(index + (1 if side else count - 1), count)
            if kind == 0:
                source = fields[g][t].at[:, BX if side else 1]
                landing = fields[g][t].at[:, 0 if side else BX + 1]
            else:
                source = edge_out.at[g, t, side]
                landing = edge_in.at[g, t, away]
            found.append(
                (
                    index < count - 1 if side else index > 0,
                    index > 0 if side else index < count - 1,
                    pltpu.make_async_remote_copy(
                        src_ref=source,
                        dst_ref=landing,
                        send_sem=send_sem.at[g, t, side, kind],
                        recv_sem=recv_sem.at[g, t, side, kind],
                        device_id={axes[g][kind]: target},
                        device_id_type=MESH,
                    ),
                )
            )
        return found

    def send(g, t, kind):
        for side in range(2):
            sends, _, copy = copies(g, t, side)[kind]
            pl.when(sends)(copy.start)

    def arrive(g, t):
        for side in range(2):
            for _, receives, copy in copies(g, t, side):
                pl.when(receives)(copy.wait_recv)

    def left(g, t):
        for side in range(2):
            for sends, _, copy in copies(g, t, side):
                pl.when(sends)(copy.wait_send)

    row = lax.broadcasted_iota(jnp.int32, (BY, BZ), 0)
    lane = lax.broadcasted_iota(jnp.int32, (BY, BZ), 1)

    def fold(x):
        return x.reshape(BY // 8, 8, BZ)

    def sweep(g, t):
        now = fields[g][t]
        source = inputs[g][2]

        def rows(x, carry):
            around, steep = [], [[], [], []]
            for c in range(NVAR):
                here = now[c, x + 1]
                x_low, x_high = now[c, x], now[c, x + 2]
                y_low = jnp.where(row == 0, edge_in[g, t, 0, c, x], pltpu.roll(here, 1, axis=0))
                y_high = jnp.where(row == BY - 1, edge_in[g, t, 1, c, x], pltpu.roll(here, BY - 1, axis=0))
                z_low = jnp.where(lane == 0, 0.0, pltpu.roll(here, 1, axis=1))
                z_high = jnp.where(lane == BZ - 1, 0.0, pltpu.roll(here, BZ - 1, axis=1))
                around.append(
                    fold((x_low + x_high) + (y_low + y_high) + (z_low + z_high) + source[c, x])
                )
                for d, (low, high) in enumerate(((x_low, x_high), (y_low, y_high), (z_low, z_high))):
                    steep[d].append(fold(slopes[g, d, x] * (low - high)))
            factor = scale[x] if g else 1.0 / 12.0
            for i in range(NVAR):
                total = around[i]
                for d in range(3):
                    for j in range(NVAR):
                        total = total - mix[(d * NVAR + j) * NVAR + i] * steep[d][j]
                total = total.reshape(BY, BZ) * factor
                if t == ITERS - 1:
                    outputs[g][i, x] = total
                else:
                    fields[g][t + 1][i, x + 1] = total
                    edge_out[g, t + 1, 0, i, x] = total[0:1]
                    edge_out[g, t + 1, 1, i, x] = total[BY - 1 : BY]
            return carry

        lax.fori_loop(0, 2, lambda k, carry: rows(k * (BX - 1), carry), 0, unroll=2)
        if t + 1 < ITERS:
            send(g, t + 1, 0)
        lax.fori_loop(1, BX - 1, rows, 0, unroll=2)
        if t + 1 < ITERS:
            send(g, t + 1, 1)

    def first_edges(g):
        def rows(x, carry):
            for c in range(NVAR):
                here = fields[g][0][c, x + 1]
                edge_out[g, 0, 0, c, x] = here[0:1]
                edge_out[g, 0, 1, c, x] = here[BY - 1 : BY]
            return carry

        lax.fori_loop(0, BX, rows, 0)

    def aligned(index, size):
        return pl.ds(pl.multiple_of(index * size, size), size)

    donors = Exchange(
        lambda v: donors_out.at[aligned(v, n_bulk * 8)],
        donors_mid,
        lambda b: donors_mid.at[:, aligned(b, 8)],
        donors_in,
        donor_sems,
    )
    for g in range(2):
        loads[g].wait()
        first_edges(g)
    for load in loads[2:]:
        load.start()
    greeted()
    for g in range(2):
        for kind in range(2):
            send(g, 0, kind)
    for k in (2, 3, 4):
        loads[k].wait()
    lax.fori_loop(0, BX, slope_rows, 0)
    loads[7].wait()
    loads[8].wait()
    for b in range(n_bulk):
        owners = pl.ds(b * n_valve, n_valve)
        for k in range(7):
            donors_out[pl.ds(b * 8 + k, n_valve, stride=n_bulk * 8), :] = weight_ref[k, owners]
        donors_out[pl.ds(b * 8 + 7, n_valve, stride=n_bulk * 8), :] = base_ref[owners].astype(f32)
    donors_mid[valve] = donors_out[aligned(valve, n_bulk * 8)]
    for d in range(3):
        for j in range(NVAR):
            for i in range(NVAR):
                mix[(d * NVAR + j) * NVAR + i] = jnp.broadcast_to(flux_ref[j, d : d + 1, i : i + 1], (8, BZ))
    for k in (5, 6, 9):
        loads[k].wait()
    for t in range(ITERS):
        arrive(0, t)
        sweep(0, t)
        if t + 1 < ITERS:
            arrive(1, t)
            sweep(1, t)

    for step in range(1, n_valve):
        donors.start_first(step)

    for c in range(NVAR):
        hi, lo = split(valve_out[c].reshape(PLANES, BZ).T)
        table[pl.ds(c * BZ, BZ), 0:PLANES] = hi
        table[pl.ds(c * BZ, BZ), PLANES : 2 * PLANES] = lo
    total[...] = jnp.zeros_like(total)
    plane_row = as_bf16(lax.broadcasted_iota(jnp.int32, (PLANES, CAP), 0))
    depth_row = lax.broadcasted_iota(jnp.int32, (BZ, CAP), 0)
    pair_row = as_bf16(lax.broadcasted_iota(jnp.int32, (PAIRS, CAP), 0))
    slot = lax.broadcasted_iota(jnp.int32, (1, CAP), 1)
    one, zero = jnp.ones((), bf16), jnp.zeros((), bf16)

    values = Exchange(
        lambda v: picked.at[v], middle, lambda b: middle.at[:, b], arrived, value_sems
    )

    def pick(part, carry):
        steps = [part * ROWS + u + 1 for u in range(ROWS)]
        rows_v = [lax.rem(valve + step, n_valve) for step in steps]
        places = [(b, v) for v in rows_v for b in range(n_bulk)]
        hits, depths = [], []
        for b, v in places:
            owner = b * n_valve + v
            cell = cell_ref[owner]
            hits.append(jnp.where(plane_row == as_bf16(cell >> 7), one, zero))
            depths.append(jnp.where(slot < count_ref[0, owner], cell & (BZ - 1), -1))
        hits = jnp.concatenate(hits, axis=1)
        columns = lax.dot_general(
            table[...], jnp.concatenate([hits, hits], axis=0), NN, preferred_element_type=f32
        )
        for u, (b, v) in enumerate(places):
            here = depth_row == depths[u]
            rows = [
                jnp.sum(
                    jnp.where(here, columns[c * BZ : (c + 1) * BZ, u * CAP : (u + 1) * CAP], 0.0),
                    axis=0,
                    keepdims=True,
                )
                for c in range(NVAR)
            ]
            picked[v, b] = jnp.concatenate(rows, axis=0)
        for step in steps:
            pl.when(step < n_valve)(lambda step=step: values.start_first(step))
        return carry

    parts = n_valve // ROWS
    lax.fori_loop(0, parts // 2, pick, 0)
    donors.finish_first()
    donors.start_second()
    for v in range(n_valve):
        donors_in[bulk, v] = donors_mid[v, aligned(bulk, 8)]
    lax.fori_loop(parts // 2, parts, pick, 0)
    middle[valve] = picked[valve]
    arrive(1, ITERS - 1)
    sweep(1, ITERS - 1)
    values.finish_first()
    values.start_second()
    for v in range(n_valve):
        arrived[bulk, v] = middle[v, bulk]

    def terms(group, sender):
        base = donors_in[group, sender, 7:8].astype(jnp.int32)
        plane = base >> 7
        odd = (base & 1) == 1
        weight = [donors_in[group, sender, k : k + 1] for k in range(7)]
        weight.append(1.0 - ((weight[0] + weight[1]) + (weight[2] + weight[3]) + (weight[4] + weight[5]) + weight[6]))
        rows = []
        for pair in range(4):
            near, deep = weight[2 * pair], weight[2 * pair + 1]
            rows += [jnp.where(odd, 0.0, near), jnp.where(odd, near, deep), jnp.where(odd, deep, 0.0)]
        weight_hi, weight_lo = split(jnp.concatenate(rows, axis=0))
        value_hi, value_lo = split(arrived[group, sender])
        hits = [plane_row == as_bf16(plane + off) for off in (0, 1, BY, BY + 1)]

        def spread(weight):
            thirds = []
            for step in range(3):
                rows = jnp.zeros((PLANES, CAP), bf16)
                for pair in range(4):
                    rows = jnp.where(hits[pair], weight[3 * pair + step : 3 * pair + step + 1], rows)
                thirds.append(rows)
            return jnp.concatenate(thirds, axis=0)

        here = pair_row == as_bf16((base & (BZ - 1)) >> 1)

        def placed(value):
            return jnp.concatenate(
                [jnp.where(here, value[c : c + 1], zero) for c in range(NVAR)], axis=0
            )

        return spread(weight_hi), spread(weight_lo), placed(value_hi), placed(value_lo)

    def push(groups):
        found = [terms(group, v) for group in groups for v in range(n_valve)]
        spread_hi, spread_lo, placed_hi, placed_lo = [
            jnp.concatenate([one[i] for one in found], axis=1) for i in range(4)
        ]
        both = lax.dot_general(
            jnp.concatenate([placed_hi, placed_lo], axis=0), spread_hi, NT, preferred_element_type=f32
        )
        low = lax.dot_general(placed_hi, spread_lo, NT, preferred_element_type=f32)
        total[...] += both[: NVAR * PAIRS] + both[NVAR * PAIRS :] + low

    def landed(step):
        group = lax.rem(bulk - step + n_bulk, n_bulk)
        donors.finish_second(group)
        values.finish_second(group)
        return group

    def push_two(pair, carry):
        push([landed(2 * pair + 1), landed(2 * pair + 2)])
        return carry

    push([bulk])
    lax.fori_loop(0, (n_bulk - 1) // 2, push_two, 0)
    if n_bulk % 2 == 0:
        push([landed(n_bulk - 1)])
    for c in range(NVAR):
        rows = pl.ds(c * PAIRS, PAIRS)
        even = total[rows, 0:PLANES] + pltpu.roll(total[rows, 2 * PLANES : 3 * PLANES], 1, axis=0)
        odd = total[rows, PLANES : 2 * PLANES]
        for half in range(PLANES // BZ):
            columns = slice(half * BZ, (half + 1) * BZ)
            mixed[half, pl.ds(0, PAIRS, stride=2), :] = even[:, columns]
            mixed[half, pl.ds(1, PAIRS, stride=2), :] = odd[:, columns]
            here = pl.ds(half * (BX // 2), BX // 2)
            bg_out[c, here] = bg_swept[c, here] + mixed[half].T.reshape(BX // 2, BY, BZ)

    values.sent()
    donors.sent()
    for t in range(ITERS):
        for g in range(2):
            left(g, t)


def whole_step(flux_mix, counts, valve_adj, bg_adj, *rest):
    whole = pl.BlockSpec(memory_space=pltpu.VMEM)
    far = pl.BlockSpec(memory_space=pltpu.HBM)
    small = pl.BlockSpec(memory_space=pltpu.SMEM)
    n_bulk, n_valve = lax.axis_size("bulk"), lax.axis_size("valve")
    out = jax.ShapeDtypeStruct(valve_adj.shape, f32)
    edges = pltpu.VMEM((2, ITERS, 2, NVAR, BX, 1, BZ), f32)
    return pl.pallas_call(
        step_kernel,
        out_shape=(out, out),
        in_specs=[whole, small] + [far] * 10,
        out_specs=(whole, whole),
        scratch_shapes=[pltpu.VMEM((NVAR, BX + 2, BY, BZ), f32)] * (2 * ITERS)
        + [
            pltpu.VMEM((2, 3, BX, BY, BZ), f32),
            pltpu.VMEM((BX, BY, BZ), f32),
            edges,
            edges,
            pltpu.VMEM((3 * NVAR * NVAR, 8, BZ), f32),
            pltpu.VMEM((n_valve * n_bulk * 8, CAP), f32),
            pltpu.VMEM((n_valve, n_bulk * 8, CAP), f32),
            pltpu.VMEM((n_bulk, n_valve, 8, CAP), f32),
            pltpu.VMEM((NVAR, BX, BY, BZ), f32),
            pltpu.VMEM((NVAR * BZ, 2 * PLANES), bf16),
            pltpu.VMEM((n_valve, n_bulk, NVAR, CAP), f32),
            pltpu.VMEM((n_valve, n_bulk, NVAR, CAP), f32),
            pltpu.VMEM((n_bulk, n_valve, NVAR, CAP), f32),
            pltpu.VMEM((NVAR * PAIRS, 3 * PLANES), f32),
            pltpu.VMEM((PLANES // BZ, BZ, BZ), f32),
        ]
        + [pltpu.VMEM(x.shape, x.dtype) for x in rest]
        + [
            pltpu.SemaphoreType.DMA((2 + len(rest),)),
            pltpu.SemaphoreType.DMA((2, ITERS, 2, 2)),
            pltpu.SemaphoreType.DMA((2, ITERS, 2, 2)),
        ]
        + exchange_sems(n_bulk, n_valve) * 2,
        compiler_params=pltpu.CompilerParams(
            collective_id=0, has_side_effects=True, vmem_limit_bytes=56 * 2**20
        ),
    )(flux_mix, counts, valve_adj, bg_adj, *rest)


def body(
    bg_adjoint,
    bg_velocity,
    bg_source,
    bg_iblank,
    valve_adjoint,
    valve_velocity,
    valve_source,
    flux_mix,
    rec_cell,
    donor_base,
    donor_weight,
    slot_count,
):
    n_owners = rec_cell.shape[1]
    valve_out, bg_out = whole_step(
        flux_mix.transpose(1, 0, 2),
        slot_count,
        valve_adjoint,
        bg_adjoint,
        valve_velocity,
        bg_velocity,
        bg_iblank,
        valve_source,
        bg_source,
        donor_weight[:, 0],
        donor_base[0],
        rec_cell.reshape(n_owners, 1, CAP),
    )
    return (bg_out, valve_out)


def solution(mesh):
    placed = (
        P(None, "bulk", "valve", None),
        P(None, "bulk", "valve", None),
        P(None, "bulk", "valve", None),
        P("bulk", "valve", None),
        P(None, "valve", "bulk", None),
        P(None, "valve", "bulk", None),
        P(None, "valve", "bulk", None),
        P(),
        P(("bulk", "valve"), None, None),
        P(("bulk", "valve"), None, None),
        P(None, ("bulk", "valve"), None, None),
        P(("bulk", "valve"), None),
    )
    return jax.shard_map(
        body,
        mesh=mesh,
        in_specs=placed,
        out_specs=(P(None, "bulk", "valve", None), P(None, "valve", "bulk", None)),
        check_vma=False,
    )
```

```python
import functools

import jax
import jax.numpy as jnp
from jax import lax
from jax.experimental import pallas as pl
from jax.experimental.pallas import tpu as pltpu
from jax.sharding import PartitionSpec as P

NVAR = 5
ITERS = 4
CAP = 128
BX = 8
BY = 32
BZ = 128
PLANES = BX * BY
PAIRS = BZ // 2
ROWS = 2

f32 = jnp.float32
bf16 = jnp.bfloat16
NT = (((1,), (1,)), ((), ()))
NN = (((1,), (0,)), ((), ()))
MESH = pl.DeviceIdType.MESH


def greet(bulk, valve):
    n_bulk, n_valve = lax.axis_size("bulk"), lax.axis_size("valve")
    barrier = pltpu.get_barrier_semaphore()
    for step in range(1, n_bulk):
        other = (lax.rem(bulk + step, n_bulk), valve)
        pl.semaphore_signal(barrier, inc=1, device_id=other, device_id_type=MESH)
    for step in range(1, n_valve):
        other = (bulk, lax.rem(valve + step, n_valve))
        pl.semaphore_signal(barrier, inc=1, device_id=other, device_id_type=MESH)


def greeted():
    pl.semaphore_wait(pltpu.get_barrier_semaphore(), lax.axis_size("bulk") + lax.axis_size("valve") - 2)


class Exchange:
    def __init__(self, source, middle, block, landed, sems):
        self.bulk, self.valve = lax.axis_index("bulk"), lax.axis_index("valve")
        self.n_bulk, self.n_valve = lax.axis_size("bulk"), lax.axis_size("valve")
        self.source, self.middle, self.block, self.landed = source, middle, block, landed
        self.sems = sems

    def first(self, v, landing):
        return pltpu.make_async_remote_copy(
            src_ref=self.source(v),
            dst_ref=self.middle.at[landing],
            send_sem=self.sems[0].at[v],
            recv_sem=self.sems[1].at[landing],
            device_id=(self.bulk, v),
            device_id_type=MESH,
        )

    def second(self, b, landing):
        return pltpu.make_async_remote_copy(
            src_ref=self.block(b),
            dst_ref=self.landed.at[landing],
            send_sem=self.sems[2].at[b],
            recv_sem=self.sems[3].at[landing],
            device_id=(b, self.valve),
            device_id_type=MESH,
        )

    def start_first(self, step):
        self.first(lax.rem(self.valve + step, self.n_valve), self.valve).start()

    def finish_first(self):
        for step in range(1, self.n_valve):
            v = lax.rem(self.valve + step, self.n_valve)
            self.first(v, v).wait_recv()

    def start_second(self):
        for step in range(1, self.n_bulk):
            self.second(lax.rem(self.bulk + step, self.n_bulk), self.bulk).start()

    def finish_second(self, b):
        self.second(b, b).wait_recv()

    def sent(self):
        for step in range(1, self.n_valve):
            v = lax.rem(self.valve + step, self.n_valve)
            self.first(v, v).wait_send()
        for step in range(1, self.n_bulk):
            b = lax.rem(self.bulk + step, self.n_bulk)
            self.second(b, b).wait_send()


def exchange_sems(n_bulk, n_valve):
    return [
        pltpu.SemaphoreType.DMA((n_valve,)),
        pltpu.SemaphoreType.DMA((n_valve,)),
        pltpu.SemaphoreType.DMA((n_bulk,)),
        pltpu.SemaphoreType.DMA((n_bulk,)),
    ]


def split(x):
    hi = x.astype(bf16)
    return hi, (x - hi.astype(f32)).astype(bf16)


def as_bf16(x):
    return x.astype(f32).astype(bf16)


def step_kernel(*refs):
    (flux_ref, count_ref, valve_adj, bg_adj) = refs[:4]
    far, (valve_out, bg_out) = refs[4:12], refs[12:14]
    fields = (refs[14 : 14 + ITERS], refs[14 + ITERS : 14 + 2 * ITERS])
    (slopes, scale, edge_in, edge_out, mix, donors_out, donors_mid, donors_in) = refs[22:30]
    (bg_swept, table, picked, middle, arrived, total, mixed) = refs[30:37]
    near = refs[37:45]
    (valve_vel, bg_vel, bg_blank, valve_src, bg_src, weight_ref, base_ref, cell_ref) = near
    (load_sem, send_sem, recv_sem) = refs[45:48]
    donor_sems, value_sems = refs[48:52], refs[52:56]
    bulk, valve = lax.axis_index("bulk"), lax.axis_index("valve")
    n_bulk, n_valve = lax.axis_size("bulk"), lax.axis_size("valve")
    place = {"bulk": (bulk, n_bulk), "valve": (valve, n_valve)}
    axes = (("valve", "bulk"), ("bulk", "valve"))
    inputs = ((valve_adj, valve_vel, valve_src), (bg_adj, bg_vel, bg_src))
    outputs = (valve_out, bg_swept)

    loads = [
        pltpu.make_async_copy(inputs[g][0], fields[g][0].at[:, pl.ds(1, BX)], load_sem.at[g])
        for g in range(2)
    ]
    for load in loads:
        load.start()
    loads += [pltpu.make_async_copy(far[k], near[k], load_sem.at[2 + k]) for k in range(len(near))]

    def clear(g, side):
        index, count = place[axes[g][0]]

        @pl.when(index == (0 if side == 0 else count - 1))
        def _():
            for t in range(ITERS):
                fields[g][t][:, (BX + 1) * side] = jnp.zeros((NVAR, BY, BZ), f32)

        index, count = place[axes[g][1]]

        @pl.when(index == (0 if side == 0 else count - 1))
        def _():
            for t in range(ITERS):
                edge_in[g, t, side] = jnp.zeros((NVAR, BX, 1, BZ), f32)

    for g in range(2):
        for side in range(2):
            clear(g, side)

    greet(bulk, valve)

    def slope_rows(x, carry):
        for g in range(2):
            parts = [inputs[g][1][d, x] for d in range(3)]
            square = parts[0] * parts[0] + parts[1] * parts[1] + parts[2] * parts[2]
            half = 0.5 * lax.rsqrt(1.0 + square)
            for d in range(3):
                slopes[g, d, x] = parts[d] * half
        scale[x] = bg_blank[x].astype(f32) * (1.0 / 12.0)
        return carry

    def copies(g, t, side):
        away = 1 - side
        found = []
        for kind in range(2):
            index, count = place[axes[g][kind]]
            target = lax.rem(index + (1 if side else count - 1), count)
            if kind == 0:
                source = fields[g][t].at[:, BX if side else 1]
                landing = fields[g][t].at[:, 0 if side else BX + 1]
            else:
                source = edge_out.at[g, t, side]
                landing = edge_in.at[g, t, away]
            found.append(
                (
                    index < count - 1 if side else index > 0,
                    index > 0 if side else index < count - 1,
                    pltpu.make_async_remote_copy(
                        src_ref=source,
                        dst_ref=landing,
                        send_sem=send_sem.at[g, t, side, kind],
                        recv_sem=recv_sem.at[g, t, side, kind],
                        device_id={axes[g][kind]: target},
                        device_id_type=MESH,
                    ),
                )
            )
        return found

    def send(g, t, kind):
        for side in range(2):
            sends, _, copy = copies(g, t, side)[kind]
            pl.when(sends)(copy.start)

    def arrive(g, t):
        for side in range(2):
            for _, receives, copy in copies(g, t, side):
                pl.when(receives)(copy.wait_recv)

    def left(g, t):
        for side in range(2):
            for sends, _, copy in copies(g, t, side):
                pl.when(sends)(copy.wait_send)

    row = lax.broadcasted_iota(jnp.int32, (BY, BZ), 0)
    lane = lax.broadcasted_iota(jnp.int32, (BY, BZ), 1)

    def fold(x):
        return x.reshape(BY // 8, 8, BZ)

    def sweep(g, t):
        now = fields[g][t]
        source = inputs[g][2]

        def rows(x, carry):
            around, steep = [], [[], [], []]
            for c in range(NVAR):
                here = now[c, x + 1]
                x_low, x_high = now[c, x], now[c, x + 2]
                y_low = jnp.where(row == 0, edge_in[g, t, 0, c, x], pltpu.roll(here, 1, axis=0))
                y_high = jnp.where(row == BY - 1, edge_in[g, t, 1, c, x], pltpu.roll(here, BY - 1, axis=0))
                z_low = jnp.where(lane == 0, 0.0, pltpu.roll(here, 1, axis=1))
                z_high = jnp.where(lane == BZ - 1, 0.0, pltpu.roll(here, BZ - 1, axis=1))
                around.append(
                    fold((x_low + x_high) + (y_low + y_high) + (z_low + z_high) + source[c, x])
                )
                for d, (low, high) in enumerate(((x_low, x_high), (y_low, y_high), (z_low, z_high))):
                    steep[d].append(fold(slopes[g, d, x] * (low - high)))
            factor = scale[x] if g else 1.0 / 12.0
            for i in range(NVAR):
                total = around[i]
                for d in range(3):
                    for j in range(NVAR):
                        total = total - mix[(d * NVAR + j) * NVAR + i] * steep[d][j]
                total = total.reshape(BY, BZ) * factor
                if t == ITERS - 1:
                    outputs[g][i, x] = total
                else:
                    fields[g][t + 1][i, x + 1] = total
                    edge_out[g, t + 1, 0, i, x] = total[0:1]
                    edge_out[g, t + 1, 1, i, x] = total[BY - 1 : BY]
            return carry

        lax.fori_loop(0, 2, lambda k, carry: rows(k * (BX - 1), carry), 0, unroll=2)
        if t + 1 < ITERS:
            send(g, t + 1, 0)
        lax.fori_loop(1, BX - 1, rows, 0, unroll=2)
        if t + 1 < ITERS:
            send(g, t + 1, 1)

    def first_edges(g):
        def rows(x, carry):
            for c in range(NVAR):
                here = fields[g][0][c, x + 1]
                edge_out[g, 0, 0, c, x] = here[0:1]
                edge_out[g, 0, 1, c, x] = here[BY - 1 : BY]
            return carry

        lax.fori_loop(0, BX, rows, 0)

    def aligned(index, size):
        return pl.ds(pl.multiple_of(index * size, size), size)

    donors = Exchange(
        lambda v: donors_out.at[aligned(v, n_bulk * 8)],
        donors_mid,
        lambda b: donors_mid.at[:, aligned(b, 8)],
        donors_in,
        donor_sems,
    )
    for g in range(2):
        loads[g].wait()
        first_edges(g)
    for load in loads[2:]:
        load.start()
    greeted()
    for g in range(2):
        for kind in range(2):
            send(g, 0, kind)
    for k in (2, 3, 4):
        loads[k].wait()
    lax.fori_loop(0, BX, slope_rows, 0)
    loads[7].wait()
    loads[8].wait()
    for b in range(n_bulk):
        owners = pl.ds(b * n_valve, n_valve)
        for k in range(7):
            donors_out[pl.ds(b * 8 + k, n_valve, stride=n_bulk * 8), :] = weight_ref[k, owners]
        donors_out[pl.ds(b * 8 + 7, n_valve, stride=n_bulk * 8), :] = base_ref[owners].astype(f32)
    donors_mid[valve] = donors_out[aligned(valve, n_bulk * 8)]
    for d in range(3):
        for j in range(NVAR):
            for i in range(NVAR):
                mix[(d * NVAR + j) * NVAR + i] = jnp.broadcast_to(flux_ref[j, d : d + 1, i : i + 1], (8, BZ))
    for k in (5, 6, 9):
        loads[k].wait()
    for t in range(ITERS):
        arrive(0, t)
        sweep(0, t)
        if t + 1 < ITERS:
            arrive(1, t)
            sweep(1, t)

    for step in range(1, n_valve):
        donors.start_first(step)

    for c in range(NVAR):
        hi, lo = split(valve_out[c].reshape(PLANES, BZ).T)
        table[pl.ds(c * BZ, BZ), 0:PLANES] = hi
        table[pl.ds(c * BZ, BZ), PLANES : 2 * PLANES] = lo
    total[...] = jnp.zeros_like(total)
    plane_row = as_bf16(lax.broadcasted_iota(jnp.int32, (PLANES, CAP), 0))
    depth_row = lax.broadcasted_iota(jnp.int32, (BZ, CAP), 0)
    pair_row = as_bf16(lax.broadcasted_iota(jnp.int32, (PAIRS, CAP), 0))
    slot = lax.broadcasted_iota(jnp.int32, (1, CAP), 1)
    one, zero = jnp.ones((), bf16), jnp.zeros((), bf16)

    values = Exchange(
        lambda v: picked.at[v], middle, lambda b: middle.at[:, b], arrived, value_sems
    )

    def pick(part, carry):
        steps = [part * ROWS + u + 1 for u in range(ROWS)]
        rows_v = [lax.rem(valve + step, n_valve) for step in steps]
        places = [(b, v) for v in rows_v for b in range(n_bulk)]
        hits, depths = [], []
        for b, v in places:
            owner = b * n_valve + v
            cell = cell_ref[owner]
            hits.append(jnp.where(plane_row == as_bf16(cell >> 7), one, zero))
            depths.append(jnp.where(slot < count_ref[0, owner], cell & (BZ - 1), -1))
        hits = jnp.concatenate(hits, axis=1)
        columns = lax.dot_general(
            table[...], jnp.concatenate([hits, hits], axis=0), NN, preferred_element_type=f32
        )
        for u, (b, v) in enumerate(places):
            here = depth_row == depths[u]
            rows = [
                jnp.sum(
                    jnp.where(here, columns[c * BZ : (c + 1) * BZ, u * CAP : (u + 1) * CAP], 0.0),
                    axis=0,
                    keepdims=True,
                )
                for c in range(NVAR)
            ]
            picked[v, b] = jnp.concatenate(rows, axis=0)
        for step in steps:
            pl.when(step < n_valve)(lambda step=step: values.start_first(step))
        return carry

    parts = n_valve // ROWS
    lax.fori_loop(0, parts // 2, pick, 0)
    donors.finish_first()
    donors.start_second()
    for v in range(n_valve):
        donors_in[bulk, v] = donors_mid[v, aligned(bulk, 8)]
    lax.fori_loop(parts // 2, parts, pick, 0)
    middle[valve] = picked[valve]
    arrive(1, ITERS - 1)
    sweep(1, ITERS - 1)
    values.finish_first()
    values.start_second()
    for v in range(n_valve):
        arrived[bulk, v] = middle[v, bulk]

    def terms(group, sender):
        base = donors_in[group, sender, 7:8].astype(jnp.int32)
        plane = base >> 7
        odd = (base & 1) == 1
        weight = [donors_in[group, sender, k : k + 1] for k in range(7)]
        weight.append(1.0 - ((weight[0] + weight[1]) + (weight[2] + weight[3]) + (weight[4] + weight[5]) + weight[6]))
        rows = []
        for pair in range(4):
            near, deep = weight[2 * pair], weight[2 * pair + 1]
            rows += [jnp.where(odd, 0.0, near), jnp.where(odd, near, deep), jnp.where(odd, deep, 0.0)]
        weight_hi, weight_lo = split(jnp.concatenate(rows, axis=0))
        value_hi, value_lo = split(arrived[group, sender])
        hits = [plane_row == as_bf16(plane + off) for off in (0, 1, BY, BY + 1)]

        def spread(weight):
            thirds = []
            for step in range(3):
                rows = jnp.zeros((PLANES, CAP), bf16)
                for pair in range(4):
                    rows = jnp.where(hits[pair], weight[3 * pair + step : 3 * pair + step + 1], rows)
                thirds.append(rows)
            return jnp.concatenate(thirds, axis=0)

        here = pair_row == as_bf16((base & (BZ - 1)) >> 1)

        def placed(value):
            return jnp.concatenate(
                [jnp.where(here, value[c : c + 1], zero) for c in range(NVAR)], axis=0
            )

        return spread(weight_hi), spread(weight_lo), placed(value_hi), placed(value_lo)

    def push(groups):
        found = [terms(group, v) for group in groups for v in range(n_valve)]
        spread_hi, spread_lo, placed_hi, placed_lo = [
            jnp.concatenate([one[i] for one in found], axis=1) for i in range(4)
        ]
        both = lax.dot_general(
            jnp.concatenate([placed_hi, placed_lo], axis=0), spread_hi, NT, preferred_element_type=f32
        )
        low = lax.dot_general(placed_hi, spread_lo, NT, preferred_element_type=f32)
        total[...] += both[: NVAR * PAIRS] + both[NVAR * PAIRS :] + low

    def landed(step):
        group = lax.rem(bulk - step + n_bulk, n_bulk)
        donors.finish_second(group)
        values.finish_second(group)
        return group

    def push_two(pair, carry):
        push([landed(2 * pair + 1), landed(2 * pair + 2)])
        return carry

    push([bulk])
    lax.fori_loop(0, (n_bulk - 1) // 2, push_two, 0)
    if n_bulk % 2 == 0:
        push([landed(n_bulk - 1)])
    for c in range(NVAR):
        rows = pl.ds(c * PAIRS, PAIRS)
        even = total[rows, 0:PLANES] + pltpu.roll(total[rows, 2 * PLANES : 3 * PLANES], 1, axis=0)
        odd = total[rows, PLANES : 2 * PLANES]
        for half in range(PLANES // BZ):
            columns = slice(half * BZ, (half + 1) * BZ)
            mixed[half, pl.ds(0, PAIRS, stride=2), :] = even[:, columns]
            mixed[half, pl.ds(1, PAIRS, stride=2), :] = odd[:, columns]
            here = pl.ds(half * (BX // 2), BX // 2)
            bg_out[c, here] = bg_swept[c, here] + mixed[half].T.reshape(BX // 2, BY, BZ)

    values.sent()
    donors.sent()
    for t in range(ITERS):
        for g in range(2):
            left(g, t)


def whole_step(flux_mix, counts, valve_adj, bg_adj, *rest):
    whole = pl.BlockSpec(memory_space=pltpu.VMEM)
    far = pl.BlockSpec(memory_space=pltpu.HBM)
    small = pl.BlockSpec(memory_space=pltpu.SMEM)
    n_bulk, n_valve = lax.axis_size("bulk"), lax.axis_size("valve")
    out = jax.ShapeDtypeStruct(valve_adj.shape, f32)
    edges = pltpu.VMEM((2, ITERS, 2, NVAR, BX, 1, BZ), f32)
    return pl.pallas_call(
        step_kernel,
        out_shape=(out, out),
        in_specs=[whole, small] + [far] * 10,
        out_specs=(whole, whole),
        scratch_shapes=[pltpu.VMEM((NVAR, BX + 2, BY, BZ), f32)] * (2 * ITERS)
        + [
            pltpu.VMEM((2, 3, BX, BY, BZ), f32),
            pltpu.VMEM((BX, BY, BZ), f32),
            edges,
            edges,
            pltpu.VMEM((3 * NVAR * NVAR, 8, BZ), f32),
            pltpu.VMEM((n_valve * n_bulk * 8, CAP), f32),
            pltpu.VMEM((n_valve, n_bulk * 8, CAP), f32),
            pltpu.VMEM((n_bulk, n_valve, 8, CAP), f32),
            pltpu.VMEM((NVAR, BX, BY, BZ), f32),
            pltpu.VMEM((NVAR * BZ, 2 * PLANES), bf16),
            pltpu.VMEM((n_valve, n_bulk, NVAR, CAP), f32),
            pltpu.VMEM((n_valve, n_bulk, NVAR, CAP), f32),
            pltpu.VMEM((n_bulk, n_valve, NVAR, CAP), f32),
            pltpu.VMEM((NVAR * PAIRS, 3 * PLANES), f32),
            pltpu.VMEM((PLANES // BZ, BZ, BZ), f32),
        ]
        + [pltpu.VMEM(x.shape, x.dtype) for x in rest]
        + [
            pltpu.SemaphoreType.DMA((2 + len(rest),)),
            pltpu.SemaphoreType.DMA((2, ITERS, 2, 2)),
            pltpu.SemaphoreType.DMA((2, ITERS, 2, 2)),
        ]
        + exchange_sems(n_bulk, n_valve) * 2,
        compiler_params=pltpu.CompilerParams(
            collective_id=0, has_side_effects=True, vmem_limit_bytes=56 * 2**20
        ),
    )(flux_mix, counts, valve_adj, bg_adj, *rest)


def hand_kernel(valve_ref, bg_ref, valve_out, bg_out, held, in_sem, out_sem):
    steps = []
    for g, (source, target) in enumerate(((valve_ref, valve_out), (bg_ref, bg_out))):
        for c in range(NVAR):
            steps.append(
                (
                    pltpu.make_async_copy(source.at[c], held.at[g, c], in_sem.at[g, c]),
                    pltpu.make_async_copy(held.at[g, c], target.at[c], out_sem.at[g, c]),
                )
            )
    for come, _ in steps:
        come.start()
    for come, go in steps:
        come.wait()
        go.start()
    for _, go in steps:
        go.wait()


def hand_over(valve, bg):
    far = pl.BlockSpec(memory_space=pl.ANY)
    out = jax.ShapeDtypeStruct(valve.shape, f32)
    return pl.pallas_call(
        hand_kernel,
        out_shape=(out, out),
        in_specs=[far, far],
        out_specs=(far, far),
        scratch_shapes=[
            pltpu.VMEM((2,) + valve.shape, f32),
            pltpu.SemaphoreType.DMA((2, NVAR)),
            pltpu.SemaphoreType.DMA((2, NVAR)),
        ],
        compiler_params=pltpu.CompilerParams(vmem_limit_bytes=56 * 2**20),
    )(valve, bg)


def body(
    bg_adjoint,
    bg_velocity,
    bg_source,
    bg_iblank,
    valve_adjoint,
    valve_velocity,
    valve_source,
    flux_mix,
    rec_cell,
    donor_base,
    donor_weight,
    slot_count,
):
    n_owners = rec_cell.shape[1]
    valve_out, bg_out = whole_step(
        flux_mix.transpose(1, 0, 2),
        slot_count,
        valve_adjoint,
        bg_adjoint,
        valve_velocity,
        bg_velocity,
        bg_iblank,
        valve_source,
        bg_source,
        donor_weight[:, 0],
        donor_base[0],
        rec_cell.reshape(n_owners, 1, CAP),
    )
    valve_out, bg_out = hand_over(valve_out, bg_out)
    return (bg_out, valve_out)


def solution(mesh):
    placed = (
        P(None, "bulk", "valve", None),
        P(None, "bulk", "valve", None),
        P(None, "bulk", "valve", None),
        P("bulk", "valve", None),
        P(None, "valve", "bulk", None),
        P(None, "valve", "bulk", None),
        P(None, "valve", "bulk", None),
        P(),
        P(("bulk", "valve"), None, None),
        P(("bulk", "valve"), None, None),
        P(None, ("bulk", "valve"), None, None),
        P(("bulk", "valve"), None),
    )
    return jax.shard_map(
        body,
        mesh=mesh,
        in_specs=placed,
        out_specs=(P(None, "bulk", "valve", None), P(None, "valve", "bulk", None)),
        check_vma=False,
    )
```
